256 devices in a mesh: roll: 16 (over z, x_hi), trans: 4 (over y), case: 4 (over x_lo, core).
Axes of the slice: x: 4 (x_hi: 2, x_lo: 2; x = x_hi * 2 + x_lo), y: 4, z: 8, core: 2. Of those that a mesh axis runs over, the one named last changes fastest.
Arguments:
- ratio_index: int32 [8], P('case'), may hold values from 0 to 15
- shifts: int32 [4], replicated, may hold values from 1 to 8, as said below
- kernel: float32 [31], replicated, may hold values from -0.06 to 0.06
- diagonal: float32 [8, 4096, 2048], P('case', 'roll', 'trans'), may hold values from 4.5 to 6
- flow_x: float32 [8, 4096, 2048], P('case', 'roll', 'trans'), may hold values from 0.1 to 0.5
- flow_y: float32 [8, 4096, 2048], P('case', 'roll', 'trans'), may hold values from 0.1 to 0.5
- pres_source: float32 [8, 4, 4096, 2048], P('case', None, 'roll', 'trans'), may hold values from -6 to 6
- rough_adjoint: float32 [8, 4096, 2048], P('case', 'roll', 'trans'), may hold values from -6 to 6
Outputs:
- pres_adjoint: float32 [8, 4096, 2048], P('case', 'roll', 'trans')
- film_adjoint: float32 [8, 4096, 2048], P('case', 'roll', 'trans')
- rough_gradient: float32 [4096, 2048], P('roll', 'trans')
The draws below stay inside these ranges and needn't reach their ends.
Inputs may be any that keep to these rules, and one draw needn't show every extreme that they name: Each step's shift is at least 1 and at most 8; some step shifts by exactly 8.
All inputs are finite; a program needn't handle non-finite values.
Results may differ from the reference program's by a relative error of at most 0.00002.
Values sent between devices are 32-bit elements; how exact they have to be, the bound alone decides.
No kernel may reach another device: no remote copies, remote signals or barrier semaphores. Data moves between devices by JAX's collectives and lax.ppermute only.
A program may use at most 128 MiB of HBM per device.

```python
import math
import jax
import jax.numpy as jnp
from jax import lax

STEPS = 4
SWEEPS = 3
KERN = 31
SMAX = 8
NSRR = 16
NX = 4096
NY = 2048
CASES = 8


def draw_shifts(key, part):
    first, second = jax.random.split(key)
    values = jax.random.randint(first, (STEPS,), 1, SMAX + 1)
    where = jax.random.randint(second, (), 0, STEPS)
    return jnp.where(jnp.arange(STEPS) == where, SMAX, values).astype(jnp.int32)


def touch_ends(entries, own_key, smallest, top_value):
    shape = entries.shape
    place = [jax.random.randint(jax.random.fold_in(own_key, axis), (), 0, shape[axis]) for axis in range(len(shape))]
    entries = entries.at[tuple(place)].set(smallest)
    longest = shape.index(max(shape))
    place[longest] = (place[longest] + 1) % shape[longest]
    return entries.at[tuple(place)].set(top_value)


def shard_levels(own_key, shape, shards, least, high):
    loudness = 1.0
    for dim, parts in shards:
        steps = jax.random.uniform(jax.random.fold_in(jax.random.fold_in(own_key, 6), dim), (parts,), jnp.float32, least / len(shards), high / len(shards))
        loudness = loudness * jnp.repeat(jnp.exp(steps), shape[dim] // parts).reshape((-1,) + (1,) * (len(shape) - 1 - dim))
    return loudness


def gaussian(key, extent, scale, limit, pieces=(), dtype=jnp.bfloat16):
    result = scale * jax.random.normal(key, extent, jnp.float32)
    if pieces:
        result = result * shard_levels(key, extent, pieces, -0.22, 0.18)
    return jnp.clip(result, -limit, limit).astype(dtype)


def setup_inputs(seed: int = 0) -> dict:
    seeds = jax.random.split(jax.random.key(seed), 9)
    ratio_index = touch_ends(jax.random.randint(seeds[0], (CASES,), 0, NSRR), jax.random.fold_in(seeds[0], 1), 0, NSRR - 1).astype(jnp.int32)
    shifts = draw_shifts(jax.random.fold_in(seeds[8], 71), 0)
    kernel = jnp.clip(jax.random.uniform(seeds[2], (KERN,), jnp.float32, -0.06, 0.06), -0.06, 0.06)
    diagonal = jnp.clip(4.5 + 1.5 * jax.random.uniform(seeds[3], (CASES, NX, NY), jnp.float32) ** shard_levels(seeds[3], (CASES, NX, NY), ((0, 4), (1, 16), (2, 4)), -0.2, 0.2), 4.5, 6.0)
    flow_x = jnp.clip(jnp.exp(math.log(0.5) - 1.609438 * jax.random.uniform(seeds[4], (CASES, NX, NY), jnp.float32) ** shard_levels(seeds[4], (CASES, NX, NY), ((0, 4), (1, 16), (2, 4)), -0.2, 0.2)), 0.1, 0.5)
    flow_y = jnp.clip(jnp.exp(math.log(0.5) - 1.609438 * jax.random.uniform(seeds[5], (CASES, NX, NY), jnp.float32) ** shard_levels(seeds[5], (CASES, NX, NY), ((0, 4), (1, 16), (2, 4)), -0.2, 0.2)), 0.1, 0.5)
    pres_source = gaussian(seeds[6], (CASES, STEPS, NX, NY), 1.0, 6.0, ((0, 4), (2, 16), (3, 4)), jnp.float32)
    rough_adjoint = gaussian(seeds[7], (CASES, NX, NY), 1.0, 6.0, ((0, 4), (1, 16), (2, 4)), jnp.float32)
    return dict(ratio_index=ratio_index, shifts=shifts, kernel=kernel, diagonal=diagonal, flow_x=flow_x, flow_y=flow_y, pres_source=pres_source, rough_adjoint=rough_adjoint)


def relax(lam, rhs, diag, fx, fy, kernel):
    half = KERN // 2
    rows = lam.shape[0]
    rolled = jnp.pad(lam, ((half, half), (0, 0)))
    conv = jnp.zeros(lam.shape, jnp.float32)
    for k in range(KERN):
        conv = conv + kernel[k] * rolled[k:k + rows]
    side = jnp.pad(lam, ((0, 0), (1, 1)))
    beside = fx * (rolled[half + 1:half + 1 + rows] + rolled[half - 1:half - 1 + rows])
    beside = beside + fy * (side[:, 2:] + side[:, :-2])
    return lam + 0.8 * (rhs - diag * lam + beside - conv) / diag


def reference(ratio_index, shifts, kernel, diagonal, flow_x, flow_y, pres_source, rough_adjoint):
    def one_case(items):
        index, diag, fx, fy, source, film = items
        ratio = 0.2 + 1.6 * index.astype(jnp.float32) / (NSRR - 1)
        lam = jnp.zeros(diag.shape, jnp.float32)
        grad = jnp.zeros(diag.shape, jnp.float32)
        for step in range(STEPS - 1, -1, -1):
            rhs = source[step] + ratio * film
            for sweep in range(SWEEPS):
                lam = relax(lam, rhs, diag, fx, fy, kernel)
            grad = grad + lam * film
            extended = jnp.concatenate([film, jnp.zeros((SMAX, film.shape[1]), jnp.float32)], axis=0)
            moved = lax.dynamic_slice_in_dim(extended, shifts[step].astype(jnp.int32), film.shape[0], 0)
            film = moved + ratio * lam
        return lam, film, grad

    lams, films, grads = lax.map(one_case, (ratio_index, diagonal, flow_x, flow_y, pres_source, rough_adjoint))
    return lams, films, jnp.sum(grads, axis=0)
```

```python
import functools

import jax
import jax.numpy as jnp
from jax import lax
from jax.experimental import pallas as pl
from jax.experimental.pallas import tpu as pltpu
from jax.sharding import PartitionSpec as P

STEPS = 4
SWEEPS = 3
KERN = 31
NSRR = 16
HALO = 48
COEF = 32
COLS = STEPS * SWEEPS - 1
BAND = 16
BLOCK = 128
SLOTS = 8

f32 = jnp.float32
bf16 = jnp.bfloat16


def banded(kern_ref, rows):
    width = rows + 2 * BAND
    shape = (rows, 3 * width)
    lane = lax.broadcasted_iota(jnp.int32, shape, 1)
    part = (lane >= width).astype(jnp.int32) + (lane >= 2 * width).astype(jnp.int32)
    tap = lane - part * width - lax.broadcasted_iota(jnp.int32, shape, 0) - 1
    value = jnp.zeros(shape, f32)
    for k in range(KERN):
        value = jnp.where(tap == k, kern_ref[k], value)
    high = value.astype(bf16).astype(f32)
    return jnp.where(part == 1, value - high, high).astype(bf16)


def pack_kernel(kern_ref, diag, fx, fy, film, src, t_big, t_mid, t_low, left, right):
    t_big[...] = banded(kern_ref, BLOCK)
    t_mid[...] = banded(kern_ref, 64)
    t_low[...] = banded(kern_ref, 32)
    cols = diag.shape[2]
    rows = 32
    lane = lax.broadcasted_iota(jnp.int32, (rows, 128), 1)

    def chunk(i, carry):
        at = pl.ds(pl.multiple_of(i * rows, rows), rows)
        for c in range(2):
            first = jnp.zeros((rows, 128), f32)
            last = jnp.zeros((rows, 128), f32)
            for slot in range(SLOTS):
                if slot < 4:
                    ref = (diag, fx, fy, film)[slot].at[c]
                else:
                    ref = src.at[c, STEPS - 1 - (slot - 4)]
                place = COLS * slot
                here = (lane >= place) & (lane < place + COLS)
                low = ref[at, 0:128]
                high = ref[at, cols - 128 : cols]
                first = jnp.where(here, pltpu.roll(low, place, 1) if place else low, first)
                last = jnp.where(here, pltpu.roll(high, (place + COLS) % 128, 1), last)
            left[c, at, :] = first
            right[c, at, :] = last
        return carry

    lax.fori_loop(0, diag.shape[1] // rows, chunk, 0)


def setup_kernel(
    ratio, flags, diag, fx, fy, film, src, from_left, from_right,
    coef, lam, film_out, extra, up1, down1, up2, down2, up3, down3,
):
    total, cols = diag.shape[1], diag.shape[2]
    rows = 16
    lane = lax.broadcasted_iota(jnp.int32, (rows, 128), 1)
    is_right = lane < COLS
    is_left = lane >= 128 - COLS
    right_ok, left_ok = flags[3], flags[2]
    inside = (is_right & (right_ok > 0)) | (is_left & (left_ok > 0))

    def chunk(i, carry):
        at = pl.ds(pl.multiple_of(i * rows, rows), rows)
        for c in range(2):
            lo = from_left[c, at, :]
            hi = from_right[c, at, :]

            def halo(slot):
                place = COLS * slot
                right = pltpu.roll(hi, (128 - place) % 128, 1) if place else hi
                left = pltpu.roll(lo, (128 - COLS - place) % 128, 1)
                return jnp.where(inside, jnp.where(is_right, right, left), 0.0)

            r = ratio[c]
            for main in (True, False):
                span = slice(0, cols) if main else slice(cols, cols + 128)
                if main:
                    w = 0.8 / diag[c, at, :]
                    x, y, h = fx[c, at, :], fy[c, at, :], film[c, at, :]
                    s = src[c, STEPS - 1, at, :]
                else:
                    d = jnp.where(inside, halo(0), 1.0)
                    w = jnp.where(inside, 0.8 / d, 0.0)
                    x, y, h, s = halo(1), halo(2), halo(3), halo(4)
                    for k in range(STEPS - 1):
                        extra[c, k, at, :] = halo(7 - k)
                coef[c, 0, at, span] = w
                coef[c, 1, at, span] = w * x
                coef[c, 2, at, span] = w * y
                film_out[c, at, span] = h
                lam[c, at, span] = w * (s + r * h)
        return carry

    lax.fori_loop(0, total // rows, chunk, 0)
    for c in range(2):
        end = total
        up1[c, 0:32, :] = lam[c, 0:32, :]
        down1[c, 0:32, :] = lam[c, end - 32 : end, :]
        for k in range(3):
            up1[c, 32 + 16 * k : 48 + 16 * k, :] = coef[c, k, 0:16, :]
            down1[c, 32 + 16 * k : 48 + 16 * k, :] = coef[c, k, end - 16 : end, :]
            up2[c, 16 * k : 16 * k + 16, :] = coef[c, k, 16:32, :]
            down2[c, 16 * k : 16 * k + 16, :] = coef[c, k, end - 32 : end - 16, :]
        up2[c, 80:136, :] = film_out[c, 0:56, :]
        down2[c, 80:112, :] = film_out[c, end - 32 : end, :]
        for ref, other, start, k in ((up2, down2, 48, 2), (up3, down3, 0, 1), (up3, down3, 32, 0)):
            to = slice(start, start + 32)
            ref[c, to, 0:cols] = src[c, k, 0:32, :]
            ref[c, to, cols : cols + 128] = extra[c, k, 0:32, :]
            other[c, to, 0:cols] = src[c, k, end - 32 : end, :]
            other[c, to, cols : cols + 128] = extra[c, k, end - 32 : end, :]


def moved(near, shift):
    stack = jnp.concatenate(near, axis=0)
    size = stack.shape[0]
    return pltpu.roll(stack, size - shift, 0)[0 : size - 8]


def split(value):
    high = value.astype(bf16)
    return high, (value - high.astype(f32)).astype(bf16)


def sweep(old, new, conv, mats, first, last, coefs, emit):
    lam, high, low = old
    start = first
    while start < last:
        size = BLOCK if last - start >= BLOCK else last - start
        near = slice(start - BAND, start + size + BAND)
        top = high[near, :]
        stack = jnp.concatenate([top, top, low[near, :]], axis=0)
        conv[0:size, :] = jnp.dot(mats[size][...], stack, preferred_element_type=f32)
        for row in range(start, start + size, 16):
            w, wx, wy, wr = coefs(row)
            area = lam[row - 8 : row + 24, :]
            mid = area[8:24]
            width = mid.shape[1]
            value = 0.2 * mid + wr
            value = value + wx * (area[7:23] + area[9:25])
            value = value + wy * (pltpu.roll(mid, 1, 1) + pltpu.roll(mid, width - 1, 1))
            value = value - w * conv[row - start : row - start + 16, :]
            emit(row, value, new)
        start += size


def keep(row, value, new):
    lam, high, low = new
    at = slice(row, row + 16)
    lam[at, :] = value
    high[at, :], low[at, :] = split(value)


def first_kernel(
    flags, t_big, t_mid, t_low, coef, lam_in, film, top, bottom,
    lam_out, up, down, grad, la, ha, oa, lb, hb, ob, conv,
):
    mats = {BLOCK: t_big, 64: t_mid, 32: t_low}
    total = lam_in.shape[1]
    cols = grad.shape[1]
    end = HALO + total
    top_ok = flags[0].astype(f32)
    low_ok = flags[1].astype(f32)

    def case(c, carry):
        for row in range(HALO - 32, end + 32, 16):
            if row < HALO:
                value = top[c, row - HALO + 32 : row - HALO + 48, :] * top_ok
            elif row >= end:
                value = bottom[c, row - end : row - end + 16, :] * low_ok
            else:
                value = lam_in[c, row - HALO : row - HALO + 16, :]
            keep(row, value, (la, ha, oa))

        def coefs(row):
            if row < HALO:
                rows = [top[c, 32 + 16 * k : 48 + 16 * k, :] * top_ok for k in range(3)]
                return (*rows, top[c, 16:32, :] * top_ok)
            if row >= end:
                rows = [bottom[c, 32 + 16 * k : 48 + 16 * k, :] * low_ok for k in range(3)]
                return (*rows, bottom[c, 0:16, :] * low_ok)
            at = slice(row - HALO, row - HALO + 16)
            return coef[c, 0, at, :], coef[c, 1, at, :], coef[c, 2, at, :], lam_in[c, at, :]

        sweep((la, ha, oa), (lb, hb, ob), conv, mats, HALO - 16, end + 16, coefs, keep)

        def emit(row, value, new):
            at = slice(row - HALO, row - HALO + 16)
            lam_out[c, at, :] = value
            if row < HALO + HALO:
                up[c, at, :] = value
            if row >= end - HALO:
                down[c, row - end + HALO : row - end + HALO + 16, :] = value
            term = value[:, 0:cols] * film[c, at, 0:cols]
            grad[at, :] = jnp.where(c == 0, term, grad[at, :] + term)

        sweep((lb, hb, ob), None, conv, mats, HALO, end, coefs, emit)
        return carry

    lax.fori_loop(0, 2, case, 0)


def step_kernel(
    step, ratio, shifts, flags, t_big, t_mid, t_low, coef, inner_top, inner_bot, outer_top, outer_bot,
    src, extra, src_top, src_bot, lam_in, lam_top, lam_bot, film, grad_in, *rest,
):
    final = step == 0
    if final:
        lam_out, film_out, grad, film_now, la, ha, oa, lb, hb, ob, wr_ref, conv = rest
    else:
        lam_out, up, down, film_now, grad, la, ha, oa, lb, hb, ob, wr_ref, conv = rest
    mats = {BLOCK: t_big, 64: t_mid, 32: t_low}
    total = lam_in.shape[1]
    cols = grad.shape[1]
    end = HALO + total
    top_ok = flags[0].astype(f32)
    low_ok = flags[1].astype(f32)
    reach = 8 * step
    place = {2: 48, 1: 0, 0: 32}[step]

    def case(c, carry):
        r = ratio[c]

        def old_film(row):
            if step == 2:
                if row < HALO:
                    return outer_top[c, 80 + row - HALO + 32 : 88 + row - HALO + 32, :] * top_ok
                if row >= end:
                    return outer_bot[c, 80 + row - end : 88 + row - end, :] * low_ok
                return film[c, row - HALO : row - HALO + 8, :]
            at = row - (HALO - COEF)
            return film[c, at : at + 8, :]

        def halo_coef(row, k):
            if row < HALO:
                ref, at = (inner_top, 32) if row >= HALO - 16 else (outer_top, 0)
                return ref[c, at + 16 * k : at + 16 * k + 16, :] * top_ok
            ref, at = (inner_bot, 32) if row < end + 16 else (outer_bot, 0)
            return ref[c, at + 16 * k : at + 16 * k + 16, :] * low_ok

        def coef_at(row, k):
            if HALO <= row < end:
                return coef[c, k, row - HALO : row - HALO + 16, :]
            return halo_coef(row, k)

        shift = shifts[step + 1]
        for row in range(0, end + HALO, 16):
            if row < HALO:
                lam = lam_top[c, row : row + 16, :] * top_ok
            elif row >= end:
                lam = lam_bot[c, row - end : row - end + 16, :] * low_ok
            else:
                lam = lam_in[c, row - HALO : row - HALO + 16, :]
            keep(row, lam, (la, ha, oa))
            if row < HALO - COEF or row >= end + COEF + reach:
                continue
            height = 16 if row + 16 <= end + COEF + reach else 8
            near = [old_film(row + k) for k in range(0, height + 8, 8)]
            now = moved(near, shift) + r * lam[0:height]
            film_now[c, row - HALO + COEF : row - HALO + COEF + height, :] = now
            if row >= end + COEF:
                continue
            w = coef_at(row, 0)
            at = row - HALO + COEF
            if row < HALO:
                wr_ref[at : at + 16, :] = w * (src_top[c, place + at : place + at + 16, :] + r * now)
            elif row >= end:
                k = place + row - end
                wr_ref[at : at + 16, :] = w * (src_bot[c, k : k + 16, :] + r * now)
            else:
                k = slice(row - HALO, row - HALO + 16)
                wr_ref[at : at + 16, 0:cols] = w[:, 0:cols] * (src[c, step, k, :] + r * now[:, 0:cols])
                wr_ref[at : at + 16, cols : cols + 128] = w[:, cols : cols + 128] * (
                    extra[c, step, k, :] + r * now[:, cols : cols + 128]
                )

        def coefs(row):
            at = row - HALO + COEF
            return coef_at(row, 0), coef_at(row, 1), coef_at(row, 2), wr_ref[at : at + 16, :]

        a, b = (la, ha, oa), (lb, hb, ob)
        sweep(a, b, conv, mats, HALO - 32, end + 32, coefs, keep)
        sweep(b, a, conv, mats, HALO - 16, end + 16, coefs, keep)

        def emit(row, value, new):
            at = slice(row - HALO, row - HALO + 16)
            here = slice(row - HALO + COEF, row - HALO + COEF + 16)
            term = value[:, 0:cols] * film_now[c, here, 0:cols]
            grad[at, :] = jnp.where(c == 0, grad_in[at, :], grad[at, :]) + term
            if final:
                lam_out[c, at, :] = value[:, 0:cols]
                near = [film_now[c, here.start + k : here.start + k + 8, 0:cols] for k in range(0, 24, 8)]
                film_out[c, at, :] = moved(near, shifts[0]) + r * value[:, 0:cols]
                return
            lam_out[c, at, :] = value
            if row < HALO + HALO:
                up[c, at, :] = value
            if row >= end - HALO:
                down[c, row - end + HALO : row - end + HALO + 16, :] = value

        sweep(a, None, conv, mats, HALO, end, coefs, emit)
        return carry

    lax.fori_loop(0, 2, case, 0)


VM = pl.BlockSpec(memory_space=pltpu.VMEM)
SM = pl.BlockSpec(memory_space=pltpu.SMEM)


def call(body, smem, vmem, outs, scratch=(), flops=0, name=None):
    moved = sum(v.size * 4 for v in vmem) + sum(4 * functools.reduce(lambda a, b: a * b, o.shape) for o in outs)
    return pl.pallas_call(
        body,
        out_shape=tuple(outs),
        in_specs=[SM] * len(smem) + [VM] * len(vmem),
        out_specs=tuple([VM] * len(outs)),
        scratch_shapes=list(scratch),
        cost_estimate=pl.CostEstimate(flops=flops, bytes_accessed=moved, transcendentals=0),
        compiler_params=pltpu.CompilerParams(vmem_limit_bytes=40 << 20),
        name=name,
    )(*smem, *vmem)


def ring(axis, step):
    count = lax.axis_size(axis)
    return [(i, (i + step) % count) for i in range(count)]


def both_ways(up, down, axis):
    from_high = lax.ppermute(up, axis, ring(axis, -1))
    from_low = lax.ppermute(down, axis, ring(axis, 1))
    return from_low, from_high


def after(values, gate):
    return lax.optimization_barrier((tuple(values), tuple(gate)))[0]


def case_sum(part):
    half = part.shape[0] // 2
    core = lax.axis_index("case") % 2
    swap_core = [(i, i ^ 1) for i in range(4)]
    swap_chip = [(i, i ^ 2) for i in range(4)]
    mine = jnp.where(core == 0, part[:half], part[half:])
    other = jnp.where(core == 0, part[half:], part[:half])
    mine = mine + lax.ppermute(other, "case", swap_core)
    mine = mine + lax.ppermute(mine, "case", swap_chip)
    other = lax.ppermute(mine, "case", swap_core)
    return jnp.where(
        core == 0, jnp.concatenate([mine, other], axis=0), jnp.concatenate([other, mine], axis=0)
    )


def on_device(ratio_index, shifts, kernel, diagonal, flow_x, flow_y, pres_source, rough_adjoint):
    ratio = 0.2 + 1.6 * ratio_index.astype(f32) / (NSRR - 1)
    cases, total, cols = diagonal.shape
    wide = cols + 128
    roll, trans = lax.axis_index("roll"), lax.axis_index("trans")
    index = jnp.arange(4)
    flags = jnp.where(
        index == 0,
        roll > 0,
        jnp.where(
            index == 1,
            roll < lax.axis_size("roll") - 1,
            jnp.where(index == 2, trans > 0, trans < lax.axis_size("trans") - 1),
        ),
    ).astype(jnp.int32)

    def shape(*dims, dtype=f32):
        return jax.ShapeDtypeStruct(dims, dtype)

    raw = (diagonal, flow_x, flow_y, rough_adjoint, pres_source)
    t_big, t_mid, t_low, left, right = call(
        pack_kernel,
        (kernel,),
        raw,
        [
            shape(BLOCK, 3 * (BLOCK + 32), dtype=bf16),
            shape(64, 3 * 96, dtype=bf16),
            shape(32, 3 * 64, dtype=bf16),
            shape(cases, total, 128),
            shape(cases, total, 128),
        ],
        name="pack",
    )
    from_left, from_right = both_ways(left, right, "trans")
    coef, lam, film, extra, up1, down1, up2, down2, up3, down3 = call(
        setup_kernel,
        (ratio, flags),
        (*raw, from_left, from_right),
        [
            shape(cases, 3, total, wide),
            shape(cases, total, wide),
            shape(cases, total, wide),
            shape(cases, STEPS - 1, total, 128),
            shape(cases, 80, wide),
            shape(cases, 80, wide),
            shape(cases, 136, wide),
            shape(cases, 112, wide),
            shape(cases, 64, wide),
            shape(cases, 64, wide),
        ],
        name="setup",
    )
    top1, bot1 = both_ways(up1, down1, "roll")
    up2, down2 = after((up2, down2), (top1, bot1))
    top2, bot2 = both_ways(up2, down2, "roll")

    rows = total + 2 * HALO
    fields = [pltpu.VMEM((rows, wide), f32), pltpu.VMEM((rows, wide), bf16), pltpu.VMEM((rows, wide), bf16)]
    conv = pltpu.VMEM((BLOCK, wide), f32)
    work = [*fields, *fields, pltpu.VMEM((total + 2 * COEF, wide), f32), conv]
    mats = (t_big, t_mid, t_low)
    state = [shape(cases, total, wide), shape(cases, HALO, wide), shape(cases, HALO, wide)]
    lam, up, down, grad = call(
        first_kernel,
        (flags,),
        (*mats, coef, lam, film, top1, bot1),
        [*state, shape(total, cols)],
        [*fields, *fields, conv],
        flops=2 << 30,
        name="first",
    )
    for step in range(STEPS - 2, -1, -1):
        lam_top, lam_bot = both_ways(up, down, "roll")
        if step == STEPS - 2:
            up3, down3 = after((up3, down3), (lam_top, lam_bot))
            top3, bot3 = both_ways(up3, down3, "roll")
        src_top, src_bot = (top2, bot2) if step == 2 else (top3, bot3)
        films = shape(cases, total + 2 * COEF + 8 * step, wide)
        if step:
            outs = [*state, films, shape(total, cols)]
            scratch = work
        else:
            outs = [shape(cases, total, cols), shape(cases, total, cols), shape(total, cols)]
            scratch = [pltpu.VMEM(films.shape, f32), *work]
        result = call(
            functools.partial(step_kernel, step),
            (ratio, shifts, flags),
            (*mats, coef, top1, bot1, top2, bot2, pres_source, extra, src_top, src_bot, lam, lam_top, lam_bot, film, grad),
            outs,
            scratch,
            flops=3 << 30,
            name="step" + str(step),
        )
        if step:
            lam, up, down, film, grad = result
        else:
            lam, film, grad = result
    return lam, film, case_sum(grad)


def solution(mesh):
    block = P("case", "roll", "trans")
    in_specs = (P("case"), P(), P(), block, block, block, P("case", None, "roll", "trans"), block)
    out_specs = (block, block, P("roll", "trans"))
    return jax.shard_map(on_device, mesh=mesh, in_specs=in_specs, out_specs=out_specs, check_vma=False)
```

```python
import functools

import jax
import jax.numpy as jnp
from jax import lax
from jax.experimental import pallas as pl
from jax.experimental.pallas import tpu as pltpu
from jax.sharding import PartitionSpec as P

STEPS = 4
SWEEPS = 3
KERN = 31
NSRR = 16
HALO = 48
COEF = 32
COLS = STEPS * SWEEPS - 1
BAND = 16
BLOCK = 128
SLOTS = 8

f32 = jnp.float32
bf16 = jnp.bfloat16


def banded(kern_ref, rows):
    width = rows + 2 * BAND
    shape = (rows, 3 * width)
    lane = lax.broadcasted_iota(jnp.int32, shape, 1)
    part = (lane >= width).astype(jnp.int32) + (lane >= 2 * width).astype(jnp.int32)
    tap = lane - part * width - lax.broadcasted_iota(jnp.int32, shape, 0) - 1
    value = jnp.zeros(shape, f32)
    for k in range(KERN):
        value = jnp.where(tap == k, kern_ref[k], value)
    high = value.astype(bf16).astype(f32)
    return jnp.where(part == 1, value - high, high).astype(bf16)


def bands_kernel(kern_ref, gate, mats):
    mats[:, 0:480] = banded(kern_ref, BLOCK)
    mats[0:64, 512:800] = banded(kern_ref, 64)
    mats[0:32, 896:1088] = banded(kern_ref, 32)


def run_copies(pairs, sems):
    copies = [pltpu.make_async_copy(a, b, sems.at[i]) for i, (a, b) in enumerate(pairs)]
    for copy in copies:
        copy.start()
    for copy in copies:
        copy.wait()


def edges_kernel(scal, diag, fx, fy, film, src, up_a, down_a, up_b, down_b, up_c, down_c, sems):
    total = diag.shape[1]
    low, high = slice(0, COEF), slice(total - COEF, total)
    pairs = []
    for edge, a, b, c in ((low, up_a, up_b, up_c), (high, down_a, down_b, down_c)):
        for k, ref in enumerate((diag, fx, fy, src.at[:, STEPS - 1], film)):
            pairs.append((ref.at[:, edge], a.at[:, 32 * k : 32 * k + 32]))
        pairs.append((src.at[:, 2, edge], b.at[:, 0:32]))
        pairs.append((src.at[:, 1, edge], c.at[:, 0:32]))
        pairs.append((src.at[:, 0, edge], c.at[:, 32:64]))
    pairs.append((film.at[:, 32:56], up_b.at[:, 32:56]))
    run_copies(pairs, sems)


def pack_kernel(scal, diag, fx, fy, film, src, left, right, low, high, sems):
    total, cols = diag.shape[1], diag.shape[2]
    refs = [diag, fx, fy, film] + [src.at[:, s] for s in (3, 2, 1, 0)]
    pairs = []
    for slot, ref in enumerate(refs):
        pairs.append((ref.at[:, :, 0:128], low.at[slot]))
        pairs.append((ref.at[:, :, cols - 128 : cols], high.at[slot]))
    run_copies(pairs, sems)
    rows = 32
    lane = lax.broadcasted_iota(jnp.int32, (rows, 128), 1)

    def chunk(i, carry):
        at = pl.ds(pl.multiple_of(i * rows, rows), rows)
        for c in range(2):
            first = jnp.zeros((rows, 128), f32)
            last = jnp.zeros((rows, 128), f32)
            for slot in range(SLOTS):
                place = COLS * slot
                here = (lane >= place) & (lane < place + COLS)
                a, b = low[slot, c, at, :], high[slot, c, at, :]
                first = jnp.where(here, pltpu.roll(a, place, 1) if place else a, first)
                last = jnp.where(here, pltpu.roll(b, (place + COLS) % 128, 1), last)
            left[c, at, :] = first
            right[c, at, :] = last
        return carry

    lax.fori_loop(0, total // rows, chunk, 0)


def ratio_of(scal, c):
    return 0.2 + 1.6 * scal[4 + c].astype(f32) / (NSRR - 1)


def main_kernel(scal, diag, fx, fy, film, src, coef, lam):
    rows = 16

    def chunk(i, carry):
        at = pl.ds(pl.multiple_of(i * rows, rows), rows)
        for c in range(2):
            w = 0.8 / diag[c, at, :]
            coef[c, 0, at, :] = w
            coef[c, 1, at, :] = w * fx[c, at, :]
            coef[c, 2, at, :] = w * fy[c, at, :]
            lam[c, at, :] = w * (src[c, STEPS - 1, at, :] + ratio_of(scal, c) * film[c, at, :])
        return carry

    lax.fori_loop(0, diag.shape[1] // rows, chunk, 0)


def side_kernel(scal, from_left, from_right, side, up, down):
    total = side.shape[2]
    rows = 32
    lane = lax.broadcasted_iota(jnp.int32, (rows, 128), 1)
    is_right = lane < COLS
    inside = (is_right & (scal[9] > 0)) | ((lane >= 128 - COLS) & (scal[8] > 0))

    def chunk(i, carry):
        at = pl.ds(pl.multiple_of(i * rows, rows), rows)
        for c in range(2):
            lo = from_left[c, at, :]
            hi = from_right[c, at, :]

            def halo(slot):
                place = COLS * slot
                right = pltpu.roll(hi, (128 - place) % 128, 1) if place else hi
                left = pltpu.roll(lo, (128 - COLS - place) % 128, 1)
                return jnp.where(inside, jnp.where(is_right, right, left), 0.0)

            w = jnp.where(inside, 0.8 / jnp.where(inside, halo(0), 1.0), 0.0)
            film = halo(3)
            side[c, 0, at, :] = w
            side[c, 1, at, :] = w * halo(1)
            side[c, 2, at, :] = w * halo(2)
            side[c, 3, at, :] = w * (halo(4) + ratio_of(scal, c) * film)
            side[c, 4, at, :] = halo(7)
            side[c, 5, at, :] = halo(6)
            side[c, 6, at, :] = halo(5)
            side[c, 7, at, :] = film
        return carry

    lax.fori_loop(0, total // rows, chunk, 0)

    def packed(c, first, at, count=4):
        result = jnp.zeros((at.stop - at.start, 128), f32)
        place = lax.broadcasted_iota(jnp.int32, result.shape, 1)
        for k in range(count):
            moved_in = pltpu.roll(side[c, first + k, at, :], 32 * k + COLS, 1)
            result = jnp.where((place >= 32 * k) & (place < 32 * k + 2 * COLS), moved_in, result)
        return result

    for c in range(2):
        for ref, at in ((up, slice(0, 32)), (down, slice(total - 32, total))):
            ref[c, 0:32, :] = packed(c, 0, at)
            ref[c, 32:64, :] = packed(c, 4, at)
            ref[c, 64:88, :] = packed(c, 7, slice(32, 56), 1)


def corner(ref, c, which, row, size):
    base, group = (64, 0) if which == 8 else (32 * (which // 4), which % 4)
    tile = ref[c, base + row : base + row + size, :]
    lane = lax.broadcasted_iota(jnp.int32, tile.shape, 1)
    tile = pltpu.roll(tile, 128 - COLS - 32 * group, 1)
    return jnp.where((lane < COLS) | (lane >= 128 - COLS), tile, 0.0)


def beside(main, extra):
    return jnp.concatenate([main, extra], axis=1)


def moved(near, shift):
    stack = jnp.concatenate(near, axis=0)
    size = stack.shape[0]
    return pltpu.roll(stack, size - shift, 0)[0 : size - 8]


def split(value):
    high = value.astype(bf16)
    return high, (value - high.astype(f32)).astype(bf16)


def matrix(mats, size):
    if size == BLOCK:
        return mats[:, 0:480]
    return mats[0:64, 512:800] if size == 64 else mats[0:32, 896:1088]


def sweep(old, new, conv, mats, first, last, coefs, emit):
    lam, high, low = old
    start = first
    while start < last:
        size = BLOCK if last - start >= BLOCK else last - start
        near = slice(start - BAND, start + size + BAND)
        top = high[near, :]
        stack = jnp.concatenate([top, top, low[near, :]], axis=0)
        conv[0:size, :] = jnp.dot(matrix(mats, size), stack, preferred_element_type=f32)
        for row in range(start, start + size, 16):
            w, wx, wy, wr = coefs(row)
            area = lam[row - 8 : row + 24, :]
            mid = area[8:24]
            width = mid.shape[1]
            value = 0.2 * mid + wr
            value = value + wx * (area[7:23] + area[9:25])
            value = value + wy * (pltpu.roll(mid, 1, 1) + pltpu.roll(mid, width - 1, 1))
            value = value - w * conv[row - start : row - start + 16, :]
            emit(row, value, new)
        start += size


def keep(row, value, new):
    lam, high, low = new
    at = slice(row, row + 16)
    lam[at, :] = value
    high[at, :], low[at, :] = split(value)


def first_kernel(
    scal, mats, coef, side, lam_in, film, top, bot, top_corner, bot_corner,
    lam_out, up, down, grad, coef_top, coef_bot, la, ha, oa, lb, hb, ob, conv,
):
    total = lam_in.shape[1]
    cols = grad.shape[1]
    end = HALO + total
    top_ok = scal[6].astype(f32)
    low_ok = scal[7].astype(f32)

    def case(c, carry):
        r = ratio_of(scal, c)
        for ref, edge, ok, out, base in (
            (top, top_corner, top_ok, coef_top, HALO - COEF),
            (bot, bot_corner, low_ok, coef_bot, end),
        ):
            for row in range(0, COEF, 16):
                w = ok * (0.8 / ref[c, row : row + 16, :])
                fx = w * ref[c, 32 + row : 48 + row, :]
                fy = w * ref[c, 64 + row : 80 + row, :]
                lam = w * (ref[c, 96 + row : 112 + row, :] + r * ref[c, 128 + row : 144 + row, :])
                for k, main in enumerate((w, fx, fy)):
                    out[c, k, row : row + 16, :] = beside(main, ok * corner(edge, c, k, row, 16))
                keep(base + row, beside(lam, ok * corner(edge, c, 3, row, 16)), (la, ha, oa))
        for row in range(HALO, end, 16):
            at = slice(row - HALO, row - HALO + 16)
            keep(row, beside(lam_in[c, at, :], side[c, 3, at, :]), (la, ha, oa))

        def coefs(row):
            if row < HALO:
                at = slice(row - HALO + COEF, row - HALO + COEF + 16)
                return (*[coef_top[c, k, at, :] for k in range(3)], None)
            if row >= end:
                at = slice(row - end, row - end + 16)
                return (*[coef_bot[c, k, at, :] for k in range(3)], None)
            at = slice(row - HALO, row - HALO + 16)
            return (*[beside(coef[c, k, at, :], side[c, k, at, :]) for k in range(3)], None)

        def with_rhs(row):
            if HALO <= row < end:
                at = slice(row - HALO, row - HALO + 16)
                return (*coefs(row)[:3], beside(lam_in[c, at, :], side[c, 3, at, :]))
            return (*coefs(row)[:3], la[row : row + 16, :])

        sweep((la, ha, oa), (lb, hb, ob), conv, mats, HALO - 16, end + 16, with_rhs, keep)

        def emit(row, value, new):
            at = slice(row - HALO, row - HALO + 16)
            lam_out[c, at, :] = value
            if row < HALO + HALO:
                up[c, at, :] = value
            if row >= end - HALO:
                down[c, row - end + HALO : row - end + HALO + 16, :] = value
            term = value[:, 0:cols] * film[c, at, :]
            grad[at, :] = jnp.where(c == 0, term, grad[at, :] + term)

        sweep((lb, hb, ob), None, conv, mats, HALO, end, with_rhs, emit)
        return carry

    lax.fori_loop(0, 2, case, 0)


def step_kernel(
    step, scal, mats, coef, side, coef_top, coef_bot, top_corner, bot_corner,
    src, src_top, src_bot, lam_in, lam_top, lam_bot, film, *rest,
):
    final = step == 0
    if step == 2:
        film_top, film_bot, *rest = rest
    grad_in, *rest = rest
    if final:
        lam_out, film_out, mine, other, film_now, grad, *rest = rest
    else:
        lam_out, up, down, film_now, grad, *rest = rest
    la, ha, oa, lb, hb, ob, wr_ref, conv = rest
    total = lam_in.shape[1]
    cols = grad.shape[1]
    end = HALO + total
    top_ok = scal[6].astype(f32)
    low_ok = scal[7].astype(f32)
    reach = 8 * step
    place = {2: 0, 1: 0, 0: 32}[step]

    def case(c, carry):
        r = ratio_of(scal, c)

        def old_film(row):
            if step < 2:
                at = row - (HALO - COEF)
                return film[c, at : at + 8, :]
            if row < HALO:
                at = row - HALO + COEF
                return top_ok * beside(film_top[c, 128 + at : 136 + at, :], corner(top_corner, c, 7, at, 8))
            if row < end:
                at = slice(row - HALO, row - HALO + 8)
                return beside(film[c, at, :], side[c, 7, at, :])
            at = row - end
            if at < 32:
                return low_ok * beside(film_bot[c, 128 + at : 136 + at, :], corner(bot_corner, c, 7, at, 8))
            return low_ok * beside(src_bot[c, at : at + 8, :], corner(bot_corner, c, 8, at - 32, 8))

        def coef_at(row, k):
            if row < HALO:
                return coef_top[c, k, row - HALO + COEF : row - HALO + COEF + 16, :]
            if row >= end:
                return coef_bot[c, k, row - end : row - end + 16, :]
            at = slice(row - HALO, row - HALO + 16)
            return beside(coef[c, k, at, :], side[c, k, at, :])

        def source(row):
            if row < HALO:
                at = row - HALO + COEF
                return beside(src_top[c, place + at : place + at + 16, :], corner(top_corner, c, 4 + step, at, 16))
            if row >= end:
                at = row - end
                return beside(src_bot[c, place + at : place + at + 16, :], corner(bot_corner, c, 4 + step, at, 16))
            at = slice(row - HALO, row - HALO + 16)
            return beside(src[c, step, at, :], side[c, 4 + step, at, :])

        shift = scal[step + 1]
        for row in range(0, end + HALO, 16):
            if row < HALO:
                lam = lam_top[c, row : row + 16, :] * top_ok
            elif row >= end:
                lam = lam_bot[c, row - end : row - end + 16, :] * low_ok
            else:
                lam = lam_in[c, row - HALO : row - HALO + 16, :]
            keep(row, lam, (la, ha, oa))
            if row < HALO - COEF or row >= end + COEF + reach:
                continue
            height = 16 if row + 16 <= end + COEF + reach else 8
            near = [old_film(row + k) for k in range(0, height + 8, 8)]
            now = moved(near, shift) + r * lam[0:height]
            at = row - HALO + COEF
            film_now[c, at : at + height, :] = now
            if row < end + COEF:
                wr_ref[at : at + 16, :] = coef_at(row, 0) * (source(row) + r * now)

        def coefs(row):
            at = row - HALO + COEF
            return coef_at(row, 0), coef_at(row, 1), coef_at(row, 2), wr_ref[at : at + 16, :]

        a, b = (la, ha, oa), (lb, hb, ob)
        sweep(a, b, conv, mats, HALO - 32, end + 32, coefs, keep)
        sweep(b, a, conv, mats, HALO - 16, end + 16, coefs, keep)

        def emit(row, value, new):
            at = slice(row - HALO, row - HALO + 16)
            here = slice(row - HALO + COEF, row - HALO + COEF + 16)
            term = value[:, 0:cols] * film_now[c, here, 0:cols]
            grad[at, :] = jnp.where(c == 0, grad_in[at, :], grad[at, :]) + term
            if final:
                lam_out[c, at, :] = value[:, 0:cols]
                near = [film_now[c, here.start + k : here.start + k + 8, 0:cols] for k in range(0, 24, 8)]
                film_out[c, at, :] = moved(near, scal[0]) + r * value[:, 0:cols]
                return
            lam_out[c, at, :] = value
            if row < HALO + HALO:
                up[c, at, :] = value
            if row >= end - HALO:
                down[c, row - end + HALO : row - end + HALO + 16, :] = value

        sweep(a, None, conv, mats, HALO, end, coefs, emit)
        return carry

    lax.fori_loop(0, 2, case, 0)
    if final:
        half = total // 2
        first = pl.multiple_of(scal[10] * half, half)
        mine[...] = grad[pl.ds(first, half), :]
        other[...] = grad[pl.ds(pl.multiple_of(half - first, half), half), :]


VM = pl.BlockSpec(memory_space=pltpu.VMEM)
SM = pl.BlockSpec(memory_space=pltpu.SMEM)
HB = pl.BlockSpec(memory_space=pltpu.HBM)


def call(body, smem, vmem, outs, scratch=(), flops=0, name=None, space=VM, limit=12):
    moved_bytes = sum(v.size * 4 for v in vmem) + sum(4 * functools.reduce(lambda a, b: a * b, o.shape) for o in outs)
    return pl.pallas_call(
        body,
        out_shape=tuple(outs),
        in_specs=[SM] * len(smem) + [space] * len(vmem),
        out_specs=tuple([VM] * len(outs)),
        scratch_shapes=list(scratch),
        cost_estimate=pl.CostEstimate(flops=flops, bytes_accessed=moved_bytes, transcendentals=0),
        compiler_params=pltpu.CompilerParams(vmem_limit_bytes=limit << 20),
        name=name,
    )(*smem, *[pltpu.with_memory_space_constraint(v, pltpu.HBM) for v in vmem] if space is HB else vmem)


def ring(axis, step):
    count = lax.axis_size(axis)
    return [(i, (i + step) % count) for i in range(count)]


def both_ways(up, down, axis):
    from_high = lax.ppermute(up, axis, ring(axis, -1))
    from_low = lax.ppermute(down, axis, ring(axis, 1))
    return from_low, from_high


def after(values, gate):
    return lax.optimization_barrier((tuple(values), tuple(gate)))[0]


def case_sum(mine, other, core):
    swap_core = [(i, i ^ 1) for i in range(4)]
    swap_chip = [(i, i ^ 2) for i in range(4)]
    mine = mine + lax.ppermute(other, "case", swap_core)
    mine = mine + lax.ppermute(mine, "case", swap_chip)
    other = lax.ppermute(mine, "case", swap_core)
    return jnp.where(
        core == 0, jnp.concatenate([mine, other], axis=0), jnp.concatenate([other, mine], axis=0)
    )


def on_device(ratio_index, shifts, kernel, diagonal, flow_x, flow_y, pres_source, rough_adjoint):
    cases, total, cols = diagonal.shape
    wide = cols + 128
    roll, trans = lax.axis_index("roll"), lax.axis_index("trans")
    core = lax.axis_index("case") % 2
    scal = jnp.concatenate(
        [
            shifts,
            ratio_index,
            jnp.stack(
                [
                    (roll > 0).astype(jnp.int32),
                    (roll < lax.axis_size("roll") - 1).astype(jnp.int32),
                    (trans > 0).astype(jnp.int32),
                    (trans < lax.axis_size("trans") - 1).astype(jnp.int32),
                    core,
                ]
            ),
        ]
    )

    def shape(*dims, dtype=f32):
        return jax.ShapeDtypeStruct(dims, dtype)

    raw = (diagonal, flow_x, flow_y, rough_adjoint, pres_source)
    up_a, down_a, up_b, down_b, up_c, down_c = call(
        edges_kernel,
        (scal,),
        raw,
        [shape(cases, rows, cols) for rows in (160, 160, 56, 32, 64, 64)],
        [pltpu.SemaphoreType.DMA((17,))],
        name="edges",
        space=HB,
    )
    top_a, bot_a = both_ways(up_a, down_a, "roll")
    tile = pltpu.VMEM((SLOTS, cases, total, 128), f32)
    left, right = call(
        pack_kernel,
        (scal,),
        raw,
        [shape(cases, total, 128)] * 2,
        [tile, tile, pltpu.SemaphoreType.DMA((2 * SLOTS,))],
        name="pack",
        space=HB,
    )
    from_left, from_right = both_ways(left, right, "trans")
    (mats,) = call(bands_kernel, (kernel,), (left,), [shape(BLOCK, 1152, dtype=bf16)], name="bands")
    coef, lam = call(
        main_kernel,
        (scal,),
        raw,
        [shape(cases, 3, total, cols), shape(cases, total, cols)],
        name="main",
    )
    from_left, from_right = after((from_left, from_right), (coef, mats))
    side, up, down = call(
        side_kernel,
        (scal,),
        (from_left, from_right),
        [shape(cases, 8, total, 128), shape(cases, 88, 128), shape(cases, 88, 128)],
        name="side",
    )
    top_corner, bot_corner = both_ways(up, down, "roll")
    up_b, down_b = after((up_b, down_b), (top_a, bot_a))
    top_b, bot_b = both_ways(up_b, down_b, "roll")

    rows = total + 2 * HALO
    fields = [pltpu.VMEM((rows, wide), f32), pltpu.VMEM((rows, wide), bf16), pltpu.VMEM((rows, wide), bf16)]
    conv = pltpu.VMEM((BLOCK, wide), f32)
    work = [*fields, *fields, pltpu.VMEM((total + 2 * COEF, wide), f32), conv]
    state = [shape(cases, total, wide), shape(cases, HALO, wide), shape(cases, HALO, wide)]
    lam, up, down, grad, coef_top, coef_bot = call(
        first_kernel,
        (scal,),
        (mats, coef, side, lam, rough_adjoint, top_a, bot_a, top_corner, bot_corner),
        [*state, shape(total, cols), shape(cases, 3, COEF, wide), shape(cases, 3, COEF, wide)],
        [*fields, *fields, conv],
        flops=2 << 30,
        name="first",
    )
    film = rough_adjoint
    for step in range(STEPS - 2, -1, -1):
        lam_top, lam_bot = both_ways(up, down, "roll")
        if step == STEPS - 2:
            up_c, down_c = after((up_c, down_c), (lam_top, lam_bot))
            top_c, bot_c = both_ways(up_c, down_c, "roll")
        src_top, src_bot = (top_b, bot_b) if step == 2 else (top_c, bot_c)
        films = shape(cases, total + 2 * COEF + 8 * step, wide)
        half = shape(total // 2, cols)
        if step:
            outs = [*state, films, shape(total, cols)]
            scratch = work
        else:
            outs = [shape(cases, total, cols), shape(cases, total, cols), half, half]
            scratch = [pltpu.VMEM(films.shape, f32), pltpu.VMEM((total, cols), f32), *work]
        more = (top_a, bot_a) if step == 2 else ()
        result = call(
            functools.partial(step_kernel, step),
            (scal,),
            (
                mats, coef, side, coef_top, coef_bot, top_corner, bot_corner, pres_source, src_top, src_bot,
                lam, lam_top, lam_bot, film, *more, grad,
            ),
            outs,
            scratch,
            flops=3 << 30,
            name="step" + str(step),
        )
        if step:
            lam, up, down, film, grad = result
        else:
            lam, film, mine, other = result
    return lam, film, case_sum(mine, other, core)


def solution(mesh):
    block = P("case", "roll", "trans")
    in_specs = (P("case"), P(), P(), block, block, block, P("case", None, "roll", "trans"), block)
    out_specs = (block, block, P("roll", "trans"))
    return jax.shard_map(on_device, mesh=mesh, in_specs=in_specs, out_specs=out_specs, check_vma=False)
```

```python
import functools

import jax
import jax.numpy as jnp
from jax import lax
from jax.experimental import pallas as pl
from jax.experimental.pallas import tpu as pltpu
from jax.sharding import PartitionSpec as P

STEPS = 4
SWEEPS = 3
KERN = 31
NSRR = 16
HALO = 48
COEF = 32
COLS = STEPS * SWEEPS - 1
BAND = 16
BLOCK = 128
SLOTS = 8

f32 = jnp.float32
bf16 = jnp.bfloat16


def banded(kern_ref, rows):
    width = rows + 2 * BAND
    shape = (rows, 3 * width)
    lane = lax.broadcasted_iota(jnp.int32, shape, 1)
    part = (lane >= width).astype(jnp.int32) + (lane >= 2 * width).astype(jnp.int32)
    tap = lane - part * width - lax.broadcasted_iota(jnp.int32, shape, 0) - 1
    value = jnp.zeros(shape, f32)
    for k in range(KERN):
        value = jnp.where(tap == k, kern_ref[k], value)
    high = value.astype(bf16).astype(f32)
    return jnp.where(part == 1, value - high, high).astype(bf16)


def bands_kernel(kern_ref, gate, mats):
    mats[:, 0:480] = banded(kern_ref, BLOCK)
    mats[0:64, 512:800] = banded(kern_ref, 64)
    mats[0:32, 896:1088] = banded(kern_ref, 32)


def run_copies(pairs, sems):
    copies = [pltpu.make_async_copy(a, b, sems.at[i]) for i, (a, b) in enumerate(pairs)]
    for copy in copies:
        copy.start()
    for copy in copies:
        copy.wait()


def edges_kernel(scal, diag, fx, fy, film, src, *rest):
    *outs, sems = rest
    total = diag.shape[1]
    low, high = slice(0, COEF), slice(total - COEF, total)
    pairs = []
    for c in range(2):
        up_a, down_a, up_b, down_b = [ref.at[c] for ref in outs]
        for edge, a, b in ((low, up_a, up_b), (high, down_a, down_b)):
            for k, ref in enumerate((diag.at[c], fx.at[c], fy.at[c], src.at[c, STEPS - 1], film.at[c])):
                pairs.append((ref.at[edge], a.at[32 * k : 32 * k + 32]))
            for k in range(STEPS - 1):
                pairs.append((src.at[c, k, edge], b.at[32 * k : 32 * k + 32]))
        pairs.append((film.at[c, 32:56], up_b.at[96:120]))
    run_copies(pairs, sems)


def pack_kernel(scal, diag, fx, fy, film, src, left, right, low, high, sems):
    total, cols = diag.shape[1], diag.shape[2]
    refs = [diag, fx, fy, film] + [src.at[:, s] for s in (3, 2, 1, 0)]
    pairs = []
    for slot, ref in enumerate(refs):
        pairs.append((ref.at[:, :, 0:128], low.at[slot]))
        pairs.append((ref.at[:, :, cols - 128 : cols], high.at[slot]))
    run_copies(pairs, sems)
    rows = 32
    lane = lax.broadcasted_iota(jnp.int32, (rows, 128), 1)

    def chunk(i, carry):
        at = pl.ds(pl.multiple_of(i * rows, rows), rows)
        for c in range(2):
            first = jnp.zeros((rows, 128), f32)
            last = jnp.zeros((rows, 128), f32)
            for slot in range(SLOTS):
                place = COLS * slot
                here = (lane >= place) & (lane < place + COLS)
                a, b = low[slot, c, at, :], high[slot, c, at, :]
                first = jnp.where(here, pltpu.roll(a, place, 1) if place else a, first)
                last = jnp.where(here, pltpu.roll(b, (place + COLS) % 128, 1), last)
            left[c, at, :] = first
            right[c, at, :] = last
        return carry

    lax.fori_loop(0, total // rows, chunk, 0)


def ratio_of(scal, c):
    return 0.2 + 1.6 * scal[4 + c].astype(f32) / (NSRR - 1)


def main_kernel(scal, diag, fx, fy, film, src, coef, lam):
    rows = 16

    def chunk(i, carry):
        at = pl.ds(pl.multiple_of(i * rows, rows), rows)
        for c in range(2):
            w = 0.8 / diag[c, at, :]
            coef[c, 0, at, :] = w
            coef[c, 1, at, :] = w * fx[c, at, :]
            coef[c, 2, at, :] = w * fy[c, at, :]
            lam[c, at, :] = w * (src[c, STEPS - 1, at, :] + ratio_of(scal, c) * film[c, at, :])
        return carry

    lax.fori_loop(0, diag.shape[1] // rows, chunk, 0)


def side_kernel(scal, from_left, from_right, side, up, down):
    total = side.shape[2]
    rows = 32
    lane = lax.broadcasted_iota(jnp.int32, (rows, 128), 1)
    is_right = lane < COLS
    inside = (is_right & (scal[9] > 0)) | ((lane >= 128 - COLS) & (scal[8] > 0))

    def chunk(i, carry):
        at = pl.ds(pl.multiple_of(i * rows, rows), rows)
        for c in range(2):
            lo = from_left[c, at, :]
            hi = from_right[c, at, :]

            def halo(slot):
                place = COLS * slot
                right = pltpu.roll(hi, (128 - place) % 128, 1) if place else hi
                left = pltpu.roll(lo, (128 - COLS - place) % 128, 1)
                return jnp.where(inside, jnp.where(is_right, right, left), 0.0)

            w = jnp.where(inside, 0.8 / jnp.where(inside, halo(0), 1.0), 0.0)
            film = halo(3)
            side[c, 0, at, :] = w
            side[c, 1, at, :] = w * halo(1)
            side[c, 2, at, :] = w * halo(2)
            side[c, 3, at, :] = w * (halo(4) + ratio_of(scal, c) * film)
            side[c, 4, at, :] = halo(7)
            side[c, 5, at, :] = halo(6)
            side[c, 6, at, :] = halo(5)
            side[c, 7, at, :] = film
        return carry

    lax.fori_loop(0, total // rows, chunk, 0)

    def packed(c, first, at, count=4):
        result = jnp.zeros((at.stop - at.start, 128), f32)
        place = lax.broadcasted_iota(jnp.int32, result.shape, 1)
        for k in range(count):
            moved_in = pltpu.roll(side[c, first + k, at, :], 32 * k + COLS, 1)
            result = jnp.where((place >= 32 * k) & (place < 32 * k + 2 * COLS), moved_in, result)
        return result

    for c in range(2):
        for ref, at in ((up, slice(0, 32)), (down, slice(total - 32, total))):
            ref[c, 0:32, :] = packed(c, 0, at)
            ref[c, 32:64, :] = packed(c, 4, at)
            ref[c, 64:88, :] = packed(c, 7, slice(32, 56), 1)


def corner(ref, c, which, row, size):
    base, group = (64, 0) if which == 8 else (32 * (which // 4), which % 4)
    tile = ref[c, base + row : base + row + size, :]
    lane = lax.broadcasted_iota(jnp.int32, tile.shape, 1)
    tile = pltpu.roll(tile, 128 - COLS - 32 * group, 1)
    return jnp.where((lane < COLS) | (lane >= 128 - COLS), tile, 0.0)


def beside(main, extra):
    return jnp.concatenate([main, extra], axis=1)


def moved(stack, shift):
    size = stack.shape[0]
    return pltpu.roll(stack, size - shift, 0)[0 : size - 8]


def span(row, size):
    return slice(row, row + size) if isinstance(row, int) else pl.ds(pl.multiple_of(row, 8), size)


def chunks(first, last, body):
    count = (last - first) // 16

    def step(i, carry):
        body(first + pl.multiple_of(i * 16, 16))
        return carry

    lax.fori_loop(0, count, step, 0, unroll=2 if count % 2 == 0 else 1)


def split(value):
    high = value.astype(bf16)
    return high, (value - high.astype(f32)).astype(bf16)


def matrix(mats, size):
    if size == BLOCK:
        return mats[:, 0:480]
    return mats[0:64, 512:800] if size == 64 else mats[0:32, 896:1088]


def sweep(old, new, conv, mats, first, last, end, coefs, emit):
    lam, high, low = old
    start = first
    while start < last:
        size = BLOCK if last - start >= BLOCK else last - start
        near = slice(start - BAND, start + size + BAND)
        top = high[near, :]
        stack = jnp.concatenate([top, top, low[near, :]], axis=0)
        conv[0:size, :] = jnp.dot(matrix(mats, size), stack, preferred_element_type=f32)

        def chunk(row, start=start):
            w, wx, wy, wr = coefs(row)
            area = lam[span(row - 8, 32), :]
            mid = area[8:24]
            width = mid.shape[1]
            value = 0.2 * mid + wr
            value = value + wx * (area[7:23] + area[9:25])
            value = value + wy * (pltpu.roll(mid, 1, 1) + pltpu.roll(mid, width - 1, 1))
            value = value - w * conv[span(row - start, 16), :]
            emit(row, value, new)

        inner, outer = max(start, HALO), min(start + size, end)
        for row in range(start, min(start + size, HALO), 16):
            chunk(row)
        if inner < outer:
            chunks(inner, outer, chunk)
        for row in range(max(start, end), start + size, 16):
            chunk(row)
        start += size


def keep(row, value, new):
    lam, high, low = new
    at = span(row, 16)
    lam[at, :] = value
    high[at, :], low[at, :] = split(value)


def send_edges(lam_out, up, down):
    total = lam_out.shape[0]
    up[...] = lam_out[0:HALO, :]
    down[...] = lam_out[total - HALO : total, :]


def first_kernel(c, scal, mats, coef, side, lam_in, film, top, bot, top_corner, bot_corner, *rest):
    if c:
        grad_in, *rest = rest
    lam_out, up, down, grad, coef_top, coef_bot, la, ha, oa, lb, hb, ob, conv = rest
    total = lam_in.shape[1]
    cols = grad.shape[1]
    end = HALO + total
    top_ok = scal[6].astype(f32)
    low_ok = scal[7].astype(f32)
    r = ratio_of(scal, c)
    for ref, edge, ok, out, base in (
        (top, top_corner, top_ok, coef_top, HALO - COEF),
        (bot, bot_corner, low_ok, coef_bot, end),
    ):
        for row in range(0, COEF, 16):
            w = ok * (0.8 / ref[c, row : row + 16, :])
            fx = w * ref[c, 32 + row : 48 + row, :]
            fy = w * ref[c, 64 + row : 80 + row, :]
            lam = w * (ref[c, 96 + row : 112 + row, :] + r * ref[c, 128 + row : 144 + row, :])
            for k, main in enumerate((w, fx, fy)):
                out[k, row : row + 16, :] = beside(main, ok * corner(edge, c, k, row, 16))
            keep(base + row, beside(lam, ok * corner(edge, c, 3, row, 16)), (la, ha, oa))

    def load(row):
        at = span(row - HALO, 16)
        keep(row, beside(lam_in[c, at, :], side[c, 3, at, :]), (la, ha, oa))

    chunks(HALO, end, load)

    def coefs(row):
        if isinstance(row, int) and not HALO <= row < end:
            ref, at = (coef_top, row - HALO + COEF) if row < HALO else (coef_bot, row - end)
            return (*[ref[k, at : at + 16, :] for k in range(3)], la[row : row + 16, :])
        at = span(row - HALO, 16)
        parts = [beside(coef[c, k, at, :], side[c, k, at, :]) for k in range(3)]
        return (*parts, beside(lam_in[c, at, :], side[c, 3, at, :]))

    sweep((la, ha, oa), (lb, hb, ob), conv, mats, HALO - 16, end + 16, end, coefs, keep)

    def emit(row, value, new):
        at = span(row - HALO, 16)
        lam_out[at, :] = value
        term = value[:, 0:cols] * film[c, at, :]
        grad[at, :] = grad_in[at, :] + term if c else term

    sweep((lb, hb, ob), None, conv, mats, HALO, end, end, coefs, emit)
    send_edges(lam_out, up, down)


def step_kernel(
    step, c, scal, mats, coef, side, coef_top, coef_bot, top_corner, bot_corner,
    src, src_top, src_bot, lam_in, lam_top, lam_bot, film, grad_in, *rest,
):
    final = step == 0
    if step == 2:
        film_top, film_bot, *rest = rest
    if final:
        if c:
            _, _, *rest = rest
            lam_full, film_full, mine, other, film_now, lam_out, film_out, grad, *rest = rest
        else:
            lam_full, film_full, grad, film_now, lam_out, film_out, *rest = rest
        sems, *rest = rest
    else:
        lam_out, up, down, film_now, grad, *rest = rest
    la, ha, oa, lb, hb, ob, wr_ref, conv = rest
    total = lam_in.shape[0]
    cols = grad.shape[1]
    end = HALO + total
    top_ok = scal[6].astype(f32)
    low_ok = scal[7].astype(f32)
    reach = 8 * step
    r = ratio_of(scal, c)

    def old_film(row, size):
        if step < 2:
            return film[span(row - (HALO - COEF), size), :]
        if not isinstance(row, int):
            at = span(row - HALO, size)
            return beside(film[c, at, :], side[c, 7, at, :])
        parts = []
        for k in range(row, row + size, 8):
            if k < HALO:
                at = k - HALO + COEF
                part = top_ok * beside(film_top[c, 128 + at : 136 + at, :], corner(top_corner, c, 7, at, 8))
            elif k < end:
                at = slice(k - HALO, k - HALO + 8)
                part = beside(film[c, at, :], side[c, 7, at, :])
            elif k < end + 32:
                at = k - end
                part = low_ok * beside(film_bot[c, 128 + at : 136 + at, :], corner(bot_corner, c, 7, at, 8))
            else:
                at = k - end - 32
                part = low_ok * beside(src_bot[c, 96 + at : 104 + at, :], corner(bot_corner, c, 8, at, 8))
            parts.append(part)
        return jnp.concatenate(parts, axis=0)

    def coef_at(row, k):
        if isinstance(row, int) and not HALO <= row < end:
            ref, at = (coef_top, row - HALO + COEF) if row < HALO else (coef_bot, row - end)
            return ref[k, at : at + 16, :]
        at = span(row - HALO, 16)
        return beside(coef[c, k, at, :], side[c, k, at, :])

    def source(row):
        if isinstance(row, int) and not HALO <= row < end:
            ref, edge, at = (src_top, top_corner, row - HALO + COEF) if row < HALO else (src_bot, bot_corner, row - end)
            here = 32 * step + at
            return beside(ref[c, here : here + 16, :], corner(edge, c, 4 + step, at, 16))
        at = span(row - HALO, 16)
        return beside(src[c, step, at, :], side[c, 4 + step, at, :])

    shift = scal[step + 1]

    def begin(row):
        if isinstance(row, int) and row < HALO:
            lam = lam_top[row : row + 16, :] * top_ok
        elif isinstance(row, int) and row >= end:
            lam = lam_bot[row - end : row - end + 16, :] * low_ok
        else:
            lam = lam_in[span(row - HALO, 16), :]
        keep(row, lam, (la, ha, oa))
        height = 16
        if isinstance(row, int):
            if row < HALO - COEF or row >= end + COEF + reach:
                return
            height = min(16, end + COEF + reach - row)
        now = moved(old_film(row, height + 8), shift) + r * lam[0:height]
        at = row - HALO + COEF
        film_now[span(at, height), :] = now
        if not isinstance(row, int) or row < end + COEF:
            wr_ref[span(at, 16), :] = coef_at(row, 0) * (source(row) + r * now)

    for row in range(0, HALO, 16):
        begin(row)
    chunks(HALO, end - 32, begin)
    for row in range(end - 32, end + HALO, 16):
        begin(row)

    def coefs(row):
        return coef_at(row, 0), coef_at(row, 1), coef_at(row, 2), wr_ref[span(row - HALO + COEF, 16), :]

    a, b = (la, ha, oa), (lb, hb, ob)
    sweep(a, b, conv, mats, HALO - 32, end + 32, end, coefs, keep)
    sweep(b, a, conv, mats, HALO - 16, end + 16, end, coefs, keep)

    def emit(row, value, new):
        at = span(row - HALO, 16)
        here = row - HALO + COEF
        grad[at, :] = grad_in[at, :] + value[:, 0:cols] * film_now[span(here, 16), 0:cols]
        if final:
            lam_out[at, :] = value[:, 0:cols]
            film_out[at, :] = moved(film_now[span(here, 24), 0:cols], scal[0]) + r * value[:, 0:cols]
        else:
            lam_out[at, :] = value

    sweep(a, None, conv, mats, HALO, end, end, coefs, emit)
    if final:
        run_copies([(lam_out, lam_full.at[c]), (film_out, film_full.at[c])], sems)
        if c:
            half = total // 2
            first = pl.multiple_of(scal[10] * half, half)
            mine[...] = grad[pl.ds(first, half), :]
            other[...] = grad[pl.ds(pl.multiple_of(half - first, half), half), :]
    else:
        send_edges(lam_out, up, down)


VM = pl.BlockSpec(memory_space=pltpu.VMEM)
SM = pl.BlockSpec(memory_space=pltpu.SMEM)
HB = pl.BlockSpec(memory_space=pltpu.HBM)


def call(body, smem, vmem, outs, scratch=(), flops=0, name=None, space=VM, limit=12, hbm_outs=0, hbm_ins=0):
    moved_bytes = sum(v.size * 4 for v in vmem) + sum(4 * functools.reduce(lambda a, b: a * b, o.shape) for o in outs)
    return pl.pallas_call(
        body,
        out_shape=tuple(outs),
        in_specs=[SM] * len(smem) + [space] * (len(vmem) - hbm_ins) + [HB] * hbm_ins,
        out_specs=tuple([HB] * hbm_outs + [VM] * (len(outs) - hbm_outs)),
        input_output_aliases={len(smem) + len(vmem) - hbm_ins + i: i for i in range(hbm_ins)},
        scratch_shapes=list(scratch),
        cost_estimate=pl.CostEstimate(flops=flops, bytes_accessed=moved_bytes, transcendentals=0),
        compiler_params=pltpu.CompilerParams(vmem_limit_bytes=limit << 20),
        name=name,
    )(*smem, *[pltpu.with_memory_space_constraint(v, pltpu.HBM) for v in vmem] if space is HB else vmem)


def ring(axis, step):
    count = lax.axis_size(axis)
    return [(i, (i + step) % count) for i in range(count)]


def both_ways(up, down, axis):
    from_high = lax.ppermute(up, axis, ring(axis, -1))
    from_low = lax.ppermute(down, axis, ring(axis, 1))
    return from_low, from_high


def after(values, gate):
    return lax.optimization_barrier((tuple(values), tuple(gate)))[0]


def case_sum(mine, other, core):
    swap_core = [(i, i ^ 1) for i in range(4)]
    swap_chip = [(i, i ^ 2) for i in range(4)]
    mine = mine + lax.ppermute(other, "case", swap_core)
    mine = mine + lax.ppermute(mine, "case", swap_chip)
    other = lax.ppermute(mine, "case", swap_core)
    return jnp.where(
        core == 0, jnp.concatenate([mine, other], axis=0), jnp.concatenate([other, mine], axis=0)
    )


def on_device(ratio_index, shifts, kernel, diagonal, flow_x, flow_y, pres_source, rough_adjoint):
    cases, total, cols = diagonal.shape
    wide = cols + 128
    roll, trans = lax.axis_index("roll"), lax.axis_index("trans")
    core = lax.axis_index("case") % 2
    scal = jnp.concatenate(
        [
            shifts,
            ratio_index,
            jnp.stack(
                [
                    (roll > 0).astype(jnp.int32),
                    (roll < lax.axis_size("roll") - 1).astype(jnp.int32),
                    (trans > 0).astype(jnp.int32),
                    (trans < lax.axis_size("trans") - 1).astype(jnp.int32),
                    core,
                ]
            ),
        ]
    )

    def shape(*dims, dtype=f32):
        return jax.ShapeDtypeStruct(dims, dtype)

    raw = (diagonal, flow_x, flow_y, rough_adjoint, pres_source)
    edges = call(
        edges_kernel,
        (scal,),
        raw,
        [shape(cases, rows, cols) for rows in (160, 160, 120, 96)],
        [pltpu.SemaphoreType.DMA((34,))],
        name="edges",
        space=HB,
    )
    near = both_ways(edges[0], edges[1], "roll")
    (scal,) = after((scal,), (edges[0],))
    tile = pltpu.VMEM((SLOTS, cases, total, 128), f32)
    left, right = call(
        pack_kernel,
        (scal,),
        raw,
        [shape(cases, total, 128)] * 2,
        [tile, tile, pltpu.SemaphoreType.DMA((2 * SLOTS,))],
        name="pack",
        space=HB,
    )
    from_left, from_right = both_ways(left, right, "trans")
    (mats,) = call(bands_kernel, (kernel,), (left,), [shape(BLOCK, 1152, dtype=bf16)], name="bands")
    coef, lam = call(
        main_kernel,
        (scal,),
        raw,
        [shape(cases, 3, total, cols), shape(cases, total, cols)],
        name="main",
    )
    from_left, from_right = after((from_left, from_right), (coef, mats))
    side, up, down = call(
        side_kernel,
        (scal,),
        (from_left, from_right),
        [shape(cases, 8, total, 128), shape(cases, 88, 128), shape(cases, 88, 128)],
        name="side",
    )
    top_corner, bot_corner = both_ways(up, down, "roll")
    rows = total + 2 * HALO
    fields = [pltpu.VMEM((rows, wide), f32), pltpu.VMEM((rows, wide), bf16), pltpu.VMEM((rows, wide), bf16)]
    conv = pltpu.VMEM((BLOCK, wide), f32)
    work = [*fields, *fields, pltpu.VMEM((total + 2 * COEF, wide), f32), conv]
    state = [shape(total, wide), shape(HALO, wide), shape(HALO, wide)]
    halo = shape(3, COEF, wide)
    block = shape(total, cols)
    grad = None
    lams, ends, coefs, films = [None] * 2, [None] * 2, [None] * 2, [rough_adjoint] * 2
    later = both_ways(*after(edges[2:4], near), "roll")
    for c in range(2):
        lams[c], up, down, grad, *coefs[c] = call(
            functools.partial(first_kernel, c),
            (scal,),
            (mats, coef, side, lam, rough_adjoint, *near, top_corner, bot_corner, *([grad] if c else [])),
            [*state, block, halo, halo],
            [*fields, *fields, conv],
            flops=1 << 30,
            name="first" + str(c),
        )
        ends[c] = both_ways(up, down, "roll")
    out = ()
    for step in range(STEPS - 2, -1, -1):
        for c in range(2):
            film = shape(total + 2 * COEF + 8 * step, wide)
            scratch = work
            hbm_outs = hbm_ins = 0
            if step:
                outs = [*state, film, block]
            else:
                full = shape(cases, total, cols)
                half = shape(total // 2, cols)
                outs = [full, full, half, half] if c else [full, full, block]
                kept = [film, block, block] + ([block] if c else [])
                scratch = [*[pltpu.VMEM(k.shape, f32) for k in kept], pltpu.SemaphoreType.DMA((2,)), *work]
                hbm_outs, hbm_ins = 2, 2 * c
            more = near if step == 2 else out
            result = call(
                functools.partial(step_kernel, step, c),
                (scal,),
                (
                    mats, coef, side, *coefs[c], top_corner, bot_corner, pres_source, *later,
                    lams[c], *ends[c], films[c], grad, *more,
                ),
                outs,
                scratch,
                flops=3 << 29,
                name="step" + str(step) + "case" + str(c),
                hbm_outs=hbm_outs,
                hbm_ins=hbm_ins,
            )
            if step:
                lams[c], up, down, films[c], grad = result
                ends[c] = both_ways(up, down, "roll")
            elif c == 0:
                *out, grad = result
            else:
                lam, film, mine, other = result
    return lam, film, case_sum(mine, other, core)


def solution(mesh):
    block = P("case", "roll", "trans")
    in_specs = (P("case"), P(), P(), block, block, block, P("case", None, "roll", "trans"), block)
    out_specs = (block, block, P("roll", "trans"))
    return jax.shard_map(on_device, mesh=mesh, in_specs=in_specs, out_specs=out_specs, check_vma=False)
```

```python
import functools

import jax
import jax.numpy as jnp
from jax import lax
from jax.experimental import pallas as pl
from jax.experimental.pallas import tpu as pltpu
from jax.sharding import PartitionSpec as P

STEPS = 4
SWEEPS = 3
KERN = 31
NSRR = 16
HALO = 48
COEF = 32
COLS = STEPS * SWEEPS - 1
BAND = 16
BLOCK = 128
SLOTS = 8

f32 = jnp.float32
bf16 = jnp.bfloat16


def banded(kern_ref, rows):
    width = rows + 2 * BAND
    shape = (rows, 3 * width)
    lane = lax.broadcasted_iota(jnp.int32, shape, 1)
    part = (lane >= width).astype(jnp.int32) + (lane >= 2 * width).astype(jnp.int32)
    tap = lane - part * width - lax.broadcasted_iota(jnp.int32, shape, 0) - 1
    value = jnp.zeros(shape, f32)
    for k in range(KERN):
        value = jnp.where(tap == k, kern_ref[k], value)
    high = value.astype(bf16).astype(f32)
    return jnp.where(part == 1, value - high, high).astype(bf16)


def bands_kernel(kern_ref, gate, mats):
    mats[:, 0:480] = banded(kern_ref, BLOCK)
    mats[0:64, 512:800] = banded(kern_ref, 64)
    mats[0:32, 896:1088] = banded(kern_ref, 32)


def run_copies(pairs, sems):
    copies = [pltpu.make_async_copy(a, b, sems.at[i]) for i, (a, b) in enumerate(pairs)]
    for copy in copies:
        copy.start()
    for copy in copies:
        copy.wait()


def edges_kernel(scal, diag, fx, fy, film, src, *rest):
    *outs, sems = rest
    total = diag.shape[1]
    low, high = slice(0, COEF), slice(total - COEF, total)
    pairs = []
    for c in range(2):
        up_a, down_a, up_b, down_b = [ref.at[c] for ref in outs]
        for edge, a, b in ((low, up_a, up_b), (high, down_a, down_b)):
            for k, ref in enumerate((diag.at[c], fx.at[c], fy.at[c], src.at[c, STEPS - 1], film.at[c])):
                pairs.append((ref.at[edge], a.at[32 * k : 32 * k + 32]))
            for k in range(STEPS - 1):
                pairs.append((src.at[c, k, edge], b.at[32 * k : 32 * k + 32]))
        pairs.append((film.at[c, 32:56], up_b.at[96:120]))
    run_copies(pairs, sems)


def pack_kernel(scal, diag, fx, fy, film, src, left, right, low, high, sems):
    total, cols = diag.shape[1], diag.shape[2]
    refs = [diag, fx, fy, film] + [src.at[:, s] for s in (3, 2, 1, 0)]
    pairs = []
    for slot, ref in enumerate(refs):
        pairs.append((ref.at[:, :, 0:128], low.at[slot]))
        pairs.append((ref.at[:, :, cols - 128 : cols], high.at[slot]))
    run_copies(pairs, sems)
    rows = 32
    lane = lax.broadcasted_iota(jnp.int32, (rows, 128), 1)

    def chunk(i, carry):
        at = pl.ds(pl.multiple_of(i * rows, rows), rows)
        for c in range(2):
            first = jnp.zeros((rows, 128), f32)
            last = jnp.zeros((rows, 128), f32)
            for slot in range(SLOTS):
                place = COLS * slot
                here = (lane >= place) & (lane < place + COLS)
                a, b = low[slot, c, at, :], high[slot, c, at, :]
                first = jnp.where(here, pltpu.roll(a, place, 1) if place else a, first)
                last = jnp.where(here, pltpu.roll(b, (place + COLS) % 128, 1), last)
            left[c, at, :] = first
            right[c, at, :] = last
        return carry

    lax.fori_loop(0, total // rows, chunk, 0)


def ratio_of(scal, c):
    return 0.2 + 1.6 * scal[4 + c].astype(f32) / (NSRR - 1)


def main_kernel(scal, diag, fx, fy, film, src, coef, lam):
    rows = 16

    def chunk(i, carry):
        at = pl.ds(pl.multiple_of(i * rows, rows), rows)
        for c in range(2):
            w = 0.8 / diag[c, at, :]
            coef[c, 0, at, :] = w
            coef[c, 1, at, :] = w * fx[c, at, :]
            coef[c, 2, at, :] = w * fy[c, at, :]
            lam[c, at, :] = w * (src[c, STEPS - 1, at, :] + ratio_of(scal, c) * film[c, at, :])
        return carry

    lax.fori_loop(0, diag.shape[1] // rows, chunk, 0)


def side_kernel(scal, from_left, from_right, side, up, down):
    total = side.shape[2]
    rows = 32
    lane = lax.broadcasted_iota(jnp.int32, (rows, 128), 1)
    is_right = lane < COLS
    inside = (is_right & (scal[9] > 0)) | ((lane >= 128 - COLS) & (scal[8] > 0))

    def chunk(i, carry):
        at = pl.ds(pl.multiple_of(i * rows, rows), rows)
        for c in range(2):
            lo = from_left[c, at, :]
            hi = from_right[c, at, :]

            def halo(slot):
                place = COLS * slot
                right = pltpu.roll(hi, (128 - place) % 128, 1) if place else hi
                left = pltpu.roll(lo, (128 - COLS - place) % 128, 1)
                return jnp.where(inside, jnp.where(is_right, right, left), 0.0)

            w = jnp.where(inside, 0.8 / jnp.where(inside, halo(0), 1.0), 0.0)
            film = halo(3)
            side[c, 0, at, :] = w
            side[c, 1, at, :] = w * halo(1)
            side[c, 2, at, :] = w * halo(2)
            side[c, 3, at, :] = w * (halo(4) + ratio_of(scal, c) * film)
            side[c, 4, at, :] = halo(7)
            side[c, 5, at, :] = halo(6)
            side[c, 6, at, :] = halo(5)
            side[c, 7, at, :] = film
        return carry

    lax.fori_loop(0, total // rows, chunk, 0)

    def packed(c, first, at, count=4):
        result = jnp.zeros((at.stop - at.start, 128), f32)
        place = lax.broadcasted_iota(jnp.int32, result.shape, 1)
        for k in range(count):
            moved_in = pltpu.roll(side[c, first + k, at, :], 32 * k + COLS, 1)
            result = jnp.where((place >= 32 * k) & (place < 32 * k + 2 * COLS), moved_in, result)
        return result

    for c in range(2):
        for ref, at in ((up, slice(0, 32)), (down, slice(total - 32, total))):
            ref[c, 0:32, :] = packed(c, 0, at)
            ref[c, 32:64, :] = packed(c, 4, at)
            ref[c, 64:88, :] = packed(c, 7, slice(32, 56), 1)


def corner(ref, c, which, row, size):
    base, group = (64, 0) if which == 8 else (32 * (which // 4), which % 4)
    tile = ref[c, base + row : base + row + size, :]
    lane = lax.broadcasted_iota(jnp.int32, tile.shape, 1)
    tile = pltpu.roll(tile, 128 - COLS - 32 * group, 1)
    return jnp.where((lane < COLS) | (lane >= 128 - COLS), tile, 0.0)


def beside(main, extra):
    return jnp.concatenate([main, extra], axis=1)


def moved(stack, shift):
    size = stack.shape[0]
    return pltpu.roll(stack, size - shift, 0)[0 : size - 8]


def span(row, size):
    return slice(row, row + size) if isinstance(row, int) else pl.ds(pl.multiple_of(row, 8), size)


def chunks(first, last, body):
    count = (last - first) // 16

    def step(i, carry):
        body(first + pl.multiple_of(i * 16, 16))
        return carry

    lax.fori_loop(0, count, step, 0, unroll=2 if count % 2 == 0 else 1)


def split(value):
    high = value.astype(bf16)
    return high, (value - high.astype(f32)).astype(bf16)


def matrix(mats, size):
    if size == BLOCK:
        return mats[:, 0:480]
    return mats[0:64, 512:800] if size == 64 else mats[0:32, 896:1088]


def sweep(old, new, conv, mats, first, last, end, coefs, emit):
    lam, high, low = old
    start = first
    while start < last:
        size = BLOCK if last - start >= BLOCK else last - start
        near = slice(start - BAND, start + size + BAND)
        top = high[near, :]
        stack = jnp.concatenate([top, top, low[near, :]], axis=0)
        conv[0:size, :] = jnp.dot(matrix(mats, size), stack, preferred_element_type=f32)

        def chunk(row, start=start):
            w, wx, wy, wr = coefs(row)
            area = lam[span(row - 8, 32), :]
            mid = area[8:24]
            width = mid.shape[1]
            value = 0.2 * mid + wr
            value = value + wx * (area[7:23] + area[9:25])
            value = value + wy * (pltpu.roll(mid, 1, 1) + pltpu.roll(mid, width - 1, 1))
            value = value - w * conv[span(row - start, 16), :]
            emit(row, value, new)

        inner, outer = max(start, HALO), min(start + size, end)
        for row in range(start, min(start + size, HALO), 16):
            chunk(row)
        for row in range(inner, outer, 16):
            chunk(row)
        for row in range(max(start, end), start + size, 16):
            chunk(row)
        start += size


def keep(row, value, new):
    lam, high, low = new
    at = span(row, 16)
    lam[at, :] = value
    high[at, :], low[at, :] = split(value)


def send_edges(lam_out, up, down):
    total = lam_out.shape[0]
    up[...] = lam_out[0:HALO, :]
    down[...] = lam_out[total - HALO : total, :]


def first_kernel(c, scal, mats, coef, side, lam_in, film, top, bot, top_corner, bot_corner, *rest):
    if c:
        grad_in, *rest = rest
    lam_out, up, down, grad, coef_top, coef_bot, la, ha, oa, lb, hb, ob, conv = rest
    total = lam_in.shape[1]
    cols = grad.shape[1]
    end = HALO + total
    top_ok = scal[6].astype(f32)
    low_ok = scal[7].astype(f32)
    r = ratio_of(scal, c)
    for ref, edge, ok, out, base in (
        (top, top_corner, top_ok, coef_top, HALO - COEF),
        (bot, bot_corner, low_ok, coef_bot, end),
    ):
        for row in range(0, COEF, 16):
            w = ok * (0.8 / ref[c, row : row + 16, :])
            fx = w * ref[c, 32 + row : 48 + row, :]
            fy = w * ref[c, 64 + row : 80 + row, :]
            lam = w * (ref[c, 96 + row : 112 + row, :] + r * ref[c, 128 + row : 144 + row, :])
            for k, main in enumerate((w, fx, fy)):
                out[k, row : row + 16, :] = beside(main, ok * corner(edge, c, k, row, 16))
            keep(base + row, beside(lam, ok * corner(edge, c, 3, row, 16)), (la, ha, oa))

    def load(row):
        at = span(row - HALO, 16)
        keep(row, beside(lam_in[c, at, :], side[c, 3, at, :]), (la, ha, oa))

    chunks(HALO, end, load)

    def coefs(row):
        if isinstance(row, int) and not HALO <= row < end:
            ref, at = (coef_top, row - HALO + COEF) if row < HALO else (coef_bot, row - end)
            return (*[ref[k, at : at + 16, :] for k in range(3)], la[row : row + 16, :])
        at = span(row - HALO, 16)
        parts = [beside(coef[c, k, at, :], side[c, k, at, :]) for k in range(3)]
        return (*parts, beside(lam_in[c, at, :], side[c, 3, at, :]))

    sweep((la, ha, oa), (lb, hb, ob), conv, mats, HALO - 16, end + 16, end, coefs, keep)

    def emit(row, value, new):
        at = span(row - HALO, 16)
        lam_out[at, :] = value
        term = value[:, 0:cols] * film[c, at, :]
        grad[at, :] = grad_in[at, :] + term if c else term

    sweep((lb, hb, ob), None, conv, mats, HALO, end, end, coefs, emit)
    send_edges(lam_out, up, down)


def step_kernel(
    step, c, scal, mats, coef, side, coef_top, coef_bot, top_corner, bot_corner,
    src, src_top, src_bot, lam_in, lam_top, lam_bot, film, grad_in, *rest,
):
    final = step == 0
    if step == 2:
        film_top, film_bot, *rest = rest
    if final:
        if c:
            _, _, *rest = rest
            lam_full, film_full, mine, other, film_now, lam_out, film_out, grad, *rest = rest
        else:
            lam_full, film_full, grad, film_now, lam_out, film_out, *rest = rest
        sems, *rest = rest
    else:
        lam_out, up, down, film_now, grad, *rest = rest
    la, ha, oa, lb, hb, ob, wr_ref, conv = rest
    total = lam_in.shape[0]
    cols = grad.shape[1]
    end = HALO + total
    top_ok = scal[6].astype(f32)
    low_ok = scal[7].astype(f32)
    reach = 8 * step
    r = ratio_of(scal, c)

    def old_film(row, size):
        if step < 2:
            return film[span(row - (HALO - COEF), size), :]
        if not isinstance(row, int):
            at = span(row - HALO, size)
            return beside(film[c, at, :], side[c, 7, at, :])
        parts = []
        for k in range(row, row + size, 8):
            if k < HALO:
                at = k - HALO + COEF
                part = top_ok * beside(film_top[c, 128 + at : 136 + at, :], corner(top_corner, c, 7, at, 8))
            elif k < end:
                at = slice(k - HALO, k - HALO + 8)
                part = beside(film[c, at, :], side[c, 7, at, :])
            elif k < end + 32:
                at = k - end
                part = low_ok * beside(film_bot[c, 128 + at : 136 + at, :], corner(bot_corner, c, 7, at, 8))
            else:
                at = k - end - 32
                part = low_ok * beside(src_bot[c, 96 + at : 104 + at, :], corner(bot_corner, c, 8, at, 8))
            parts.append(part)
        return jnp.concatenate(parts, axis=0)

    def coef_at(row, k):
        if isinstance(row, int) and not HALO <= row < end:
            ref, at = (coef_top, row - HALO + COEF) if row < HALO else (coef_bot, row - end)
            return ref[k, at : at + 16, :]
        at = span(row - HALO, 16)
        return beside(coef[c, k, at, :], side[c, k, at, :])

    def source(row):
        if isinstance(row, int) and not HALO <= row < end:
            ref, edge, at = (src_top, top_corner, row - HALO + COEF) if row < HALO else (src_bot, bot_corner, row - end)
            here = 32 * step + at
            return beside(ref[c, here : here + 16, :], corner(edge, c, 4 + step, at, 16))
        at = span(row - HALO, 16)
        return beside(src[c, step, at, :], side[c, 4 + step, at, :])

    shift = scal[step + 1]

    def begin(row):
        if isinstance(row, int) and row < HALO:
            lam = lam_top[row : row + 16, :] * top_ok
        elif isinstance(row, int) and row >= end:
            lam = lam_bot[row - end : row - end + 16, :] * low_ok
        else:
            lam = lam_in[span(row - HALO, 16), :]
        keep(row, lam, (la, ha, oa))
        height = 16
        if isinstance(row, int):
            if row < HALO - COEF or row >= end + COEF + reach:
                return
            height = min(16, end + COEF + reach - row)
        now = moved(old_film(row, height + 8), shift) + r * lam[0:height]
        at = row - HALO + COEF
        film_now[span(at, height), :] = now
        if not isinstance(row, int) or row < end + COEF:
            wr_ref[span(at, 16), :] = coef_at(row, 0) * (source(row) + r * now)

    for row in range(0, HALO, 16):
        begin(row)
    chunks(HALO, end - 32, begin)
    for row in range(end - 32, end + HALO, 16):
        begin(row)

    def coefs(row):
        return coef_at(row, 0), coef_at(row, 1), coef_at(row, 2), wr_ref[span(row - HALO + COEF, 16), :]

    a, b = (la, ha, oa), (lb, hb, ob)
    sweep(a, b, conv, mats, HALO - 32, end + 32, end, coefs, keep)
    sweep(b, a, conv, mats, HALO - 16, end + 16, end, coefs, keep)

    def emit(row, value, new):
        at = span(row - HALO, 16)
        here = row - HALO + COEF
        grad[at, :] = grad_in[at, :] + value[:, 0:cols] * film_now[span(here, 16), 0:cols]
        if final:
            lam_out[at, :] = value[:, 0:cols]
            film_out[at, :] = moved(film_now[span(here, 24), 0:cols], scal[0]) + r * value[:, 0:cols]
        else:
            lam_out[at, :] = value

    sweep(a, None, conv, mats, HALO, end, end, coefs, emit)
    if final:
        run_copies([(lam_out, lam_full.at[c]), (film_out, film_full.at[c])], sems)
        if c:
            half = total // 2
            first = pl.multiple_of(scal[10] * half, half)
            mine[...] = grad[pl.ds(first, half), :]
            other[...] = grad[pl.ds(pl.multiple_of(half - first, half), half), :]
    else:
        send_edges(lam_out, up, down)


VM = pl.BlockSpec(memory_space=pltpu.VMEM)
SM = pl.BlockSpec(memory_space=pltpu.SMEM)
HB = pl.BlockSpec(memory_space=pltpu.HBM)


def call(body, smem, vmem, outs, scratch=(), flops=0, name=None, space=VM, limit=12, hbm_outs=0, hbm_ins=0):
    moved_bytes = sum(v.size * 4 for v in vmem) + sum(4 * functools.reduce(lambda a, b: a * b, o.shape) for o in outs)
    return pl.pallas_call(
        body,
        out_shape=tuple(outs),
        in_specs=[SM] * len(smem) + [space] * (len(vmem) - hbm_ins) + [HB] * hbm_ins,
        out_specs=tuple([HB] * hbm_outs + [VM] * (len(outs) - hbm_outs)),
        input_output_aliases={len(smem) + len(vmem) - hbm_ins + i: i for i in range(hbm_ins)},
        scratch_shapes=list(scratch),
        cost_estimate=pl.CostEstimate(flops=flops, bytes_accessed=moved_bytes, transcendentals=0),
        compiler_params=pltpu.CompilerParams(vmem_limit_bytes=limit << 20),
        name=name,
    )(*smem, *[pltpu.with_memory_space_constraint(v, pltpu.HBM) for v in vmem] if space is HB else vmem)


def ring(axis, step):
    count = lax.axis_size(axis)
    return [(i, (i + step) % count) for i in range(count)]


def both_ways(up, down, axis):
    from_high = lax.ppermute(up, axis, ring(axis, -1))
    from_low = lax.ppermute(down, axis, ring(axis, 1))
    return from_low, from_high


def after(values, gate):
    return lax.optimization_barrier((tuple(values), tuple(gate)))[0]


def case_sum(mine, other, core):
    swap_core = [(i, i ^ 1) for i in range(4)]
    swap_chip = [(i, i ^ 2) for i in range(4)]
    mine = mine + lax.ppermute(other, "case", swap_core)
    mine = mine + lax.ppermute(mine, "case", swap_chip)
    other = lax.ppermute(mine, "case", swap_core)
    return jnp.where(
        core == 0, jnp.concatenate([mine, other], axis=0), jnp.concatenate([other, mine], axis=0)
    )


def on_device(ratio_index, shifts, kernel, diagonal, flow_x, flow_y, pres_source, rough_adjoint):
    cases, total, cols = diagonal.shape
    wide = cols + 128
    roll, trans = lax.axis_index("roll"), lax.axis_index("trans")
    core = lax.axis_index("case") % 2
    scal = jnp.concatenate(
        [
            shifts,
            ratio_index,
            jnp.stack(
                [
                    (roll > 0).astype(jnp.int32),
                    (roll < lax.axis_size("roll") - 1).astype(jnp.int32),
                    (trans > 0).astype(jnp.int32),
                    (trans < lax.axis_size("trans") - 1).astype(jnp.int32),
                    core,
                ]
            ),
        ]
    )

    def shape(*dims, dtype=f32):
        return jax.ShapeDtypeStruct(dims, dtype)

    raw = (diagonal, flow_x, flow_y, rough_adjoint, pres_source)
    edges = call(
        edges_kernel,
        (scal,),
        raw,
        [shape(cases, rows, cols) for rows in (160, 160, 120, 96)],
        [pltpu.SemaphoreType.DMA((34,))],
        name="edges",
        space=HB,
    )
    near = both_ways(edges[0], edges[1], "roll")
    (scal,) = after((scal,), (edges[0],))
    tile = pltpu.VMEM((SLOTS, cases, total, 128), f32)
    left, right = call(
        pack_kernel,
        (scal,),
        raw,
        [shape(cases, total, 128)] * 2,
        [tile, tile, pltpu.SemaphoreType.DMA((2 * SLOTS,))],
        name="pack",
        space=HB,
    )
    from_left, from_right = both_ways(left, right, "trans")
    (mats,) = call(bands_kernel, (kernel,), (left,), [shape(BLOCK, 1152, dtype=bf16)], name="bands")
    coef, lam = call(
        main_kernel,
        (scal,),
        raw,
        [shape(cases, 3, total, cols), shape(cases, total, cols)],
        name="main",
    )
    from_left, from_right = after((from_left, from_right), (coef, mats))
    side, up, down = call(
        side_kernel,
        (scal,),
        (from_left, from_right),
        [shape(cases, 8, total, 128), shape(cases, 88, 128), shape(cases, 88, 128)],
        name="side",
    )
    top_corner, bot_corner = both_ways(up, down, "roll")
    rows = total + 2 * HALO
    fields = [pltpu.VMEM((rows, wide), f32), pltpu.VMEM((rows, wide), bf16), pltpu.VMEM((rows, wide), bf16)]
    conv = pltpu.VMEM((BLOCK, wide), f32)
    work = [*fields, *fields, pltpu.VMEM((total + 2 * COEF, wide), f32), conv]
    state = [shape(total, wide), shape(HALO, wide), shape(HALO, wide)]
    halo = shape(3, COEF, wide)
    block = shape(total, cols)
    grad = None
    lams, ends, coefs, films = [None] * 2, [None] * 2, [None] * 2, [rough_adjoint] * 2
    later = both_ways(*after(edges[2:4], (*near, top_corner, bot_corner)), "roll")
    for c in range(2):
        lams[c], up, down, grad, *coefs[c] = call(
            functools.partial(first_kernel, c),
            (scal,),
            (mats, coef, side, lam, rough_adjoint, *near, top_corner, bot_corner, *([grad] if c else [])),
            [*state, block, halo, halo],
            [*fields, *fields, conv],
            flops=1 << 30,
            name="first" + str(c),
        )
        ends[c] = both_ways(up, down, "roll")
    out = ()
    for step in range(STEPS - 2, -1, -1):
        for c in range(2):
            film = shape(total + 2 * COEF + 8 * step, wide)
            scratch = work
            hbm_outs = hbm_ins = 0
            if step:
                outs = [*state, film, block]
            else:
                full = shape(cases, total, cols)
                half = shape(total // 2, cols)
                outs = [full, full, half, half] if c else [full, full, block]
                kept = [film, block, block] + ([block] if c else [])
                scratch = [*[pltpu.VMEM(k.shape, f32) for k in kept], pltpu.SemaphoreType.DMA((2,)), *work]
                hbm_outs, hbm_ins = 2, 2 * c
            more = near if step == 2 else out
            result = call(
                functools.partial(step_kernel, step, c),
                (scal,),
                (
                    mats, coef, side, *coefs[c], top_corner, bot_corner, pres_source, *later,
                    lams[c], *ends[c], films[c], grad, *more,
                ),
                outs,
                scratch,
                flops=3 << 29,
                name="step" + str(step) + "case" + str(c),
                hbm_outs=hbm_outs,
                hbm_ins=hbm_ins,
            )
            if step:
                lams[c], up, down, films[c], grad = result
                ends[c] = both_ways(up, down, "roll")
            elif c == 0:
                *out, grad = result
            else:
                lam, film, mine, other = result
    return lam, film, case_sum(mine, other, core)


def solution(mesh):
    block = P("case", "roll", "trans")
    in_specs = (P("case"), P(), P(), block, block, block, P("case", None, "roll", "trans"), block)
    out_specs = (block, block, P("roll", "trans"))
    return jax.shard_map(on_device, mesh=mesh, in_specs=in_specs, out_specs=out_specs, check_vma=False)
```

```python
import functools

import jax
import jax.numpy as jnp
from jax import lax
from jax.experimental import pallas as pl
from jax.experimental.pallas import tpu as pltpu
from jax.sharding import PartitionSpec as P

STEPS = 4
SWEEPS = 3
KERN = 31
NSRR = 16
HALO = 48
COEF = 32
COLS = STEPS * SWEEPS - 1
BAND = 16
BLOCK = 128
SLOTS = 8

f32 = jnp.float32
bf16 = jnp.bfloat16


def banded(kern_ref, rows):
    width = rows + 2 * BAND
    shape = (rows, 3 * width)
    lane = lax.broadcasted_iota(jnp.int32, shape, 1)
    part = (lane >= width).astype(jnp.int32) + (lane >= 2 * width).astype(jnp.int32)
    tap = lane - part * width - lax.broadcasted_iota(jnp.int32, shape, 0) - 1
    value = jnp.zeros(shape, f32)
    for k in range(KERN):
        value = jnp.where(tap == k, kern_ref[k], value)
    high = value.astype(bf16).astype(f32)
    return jnp.where(part == 1, value - high, high).astype(bf16)


def bands_kernel(kern_ref, gate, mats):
    mats[:, 0:480] = banded(kern_ref, BLOCK)
    mats[0:64, 512:800] = banded(kern_ref, 64)
    mats[0:32, 896:1088] = banded(kern_ref, 32)


def run_copies(pairs, sems):
    copies = [pltpu.make_async_copy(a, b, sems.at[i]) for i, (a, b) in enumerate(pairs)]
    for copy in copies:
        copy.start()
    for copy in copies:
        copy.wait()


def edges_kernel(scal, diag, fx, fy, film, src, *rest):
    *outs, sems = rest
    total = diag.shape[1]
    low, high = slice(0, COEF), slice(total - COEF, total)
    pairs = []
    for c in range(2):
        up_a, down_a, up_b, down_b, up_c, down_c = [ref.at[c] for ref in outs]
        for edge, a, b, d in ((low, up_a, up_b, up_c), (high, down_a, down_b, down_c)):
            for k, ref in enumerate((diag.at[c], fx.at[c], fy.at[c], src.at[c, STEPS - 1], film.at[c])):
                pairs.append((ref.at[edge], a.at[32 * k : 32 * k + 32]))
            pairs.append((src.at[c, 2, edge], b.at[0:32]))
            for k in range(STEPS - 2):
                pairs.append((src.at[c, k, edge], d.at[32 * k : 32 * k + 32]))
        pairs.append((film.at[c, 32:56], up_b.at[32:56]))
    run_copies(pairs, sems)


def pack_kernel(scal, diag, fx, fy, film, src, left, right, low, high, sems):
    total, cols = diag.shape[1], diag.shape[2]
    refs = [diag, fx, fy, film] + [src.at[:, s] for s in (3, 2, 1, 0)]
    pairs = []
    for slot, ref in enumerate(refs):
        pairs.append((ref.at[:, :, 0:128], low.at[slot]))
        pairs.append((ref.at[:, :, cols - 128 : cols], high.at[slot]))
    run_copies(pairs, sems)
    rows = 32
    lane = lax.broadcasted_iota(jnp.int32, (rows, 128), 1)

    def chunk(i, carry):
        at = pl.ds(pl.multiple_of(i * rows, rows), rows)
        for c in range(2):
            first = jnp.zeros((rows, 128), f32)
            last = jnp.zeros((rows, 128), f32)
            for slot in range(SLOTS):
                place = COLS * slot
                here = (lane >= place) & (lane < place + COLS)
                a, b = low[slot, c, at, :], high[slot, c, at, :]
                first = jnp.where(here, pltpu.roll(a, place, 1) if place else a, first)
                last = jnp.where(here, pltpu.roll(b, (place + COLS) % 128, 1), last)
            left[c, at, :] = first
            right[c, at, :] = last
        return carry

    lax.fori_loop(0, total // rows, chunk, 0)


def ratio_of(scal, c):
    return 0.2 + 1.6 * scal[4 + c].astype(f32) / (NSRR - 1)


def main_kernel(scal, diag, fx, fy, film, src, coef, lam):
    rows = 16

    def chunk(i, carry):
        at = pl.ds(pl.multiple_of(i * rows, rows), rows)
        for c in range(2):
            w = 0.8 / diag[c, at, :]
            coef[c, 0, at, :] = w
            coef[c, 1, at, :] = w * fx[c, at, :]
            coef[c, 2, at, :] = w * fy[c, at, :]
            lam[c, at, :] = w * (src[c, STEPS - 1, at, :] + ratio_of(scal, c) * film[c, at, :])
        return carry

    lax.fori_loop(0, diag.shape[1] // rows, chunk, 0)


def side_kernel(scal, from_left, from_right, side, up, down):
    total = side.shape[2]
    rows = 32
    lane = lax.broadcasted_iota(jnp.int32, (rows, 128), 1)
    is_right = lane < COLS
    inside = (is_right & (scal[9] > 0)) | ((lane >= 128 - COLS) & (scal[8] > 0))

    def chunk(i, carry):
        at = pl.ds(pl.multiple_of(i * rows, rows), rows)
        for c in range(2):
            lo = from_left[c, at, :]
            hi = from_right[c, at, :]

            def halo(slot):
                place = COLS * slot
                right = pltpu.roll(hi, (128 - place) % 128, 1) if place else hi
                left = pltpu.roll(lo, (128 - COLS - place) % 128, 1)
                return jnp.where(inside, jnp.where(is_right, right, left), 0.0)

            w = jnp.where(inside, 0.8 / jnp.where(inside, halo(0), 1.0), 0.0)
            film = halo(3)
            side[c, 0, at, :] = w
            side[c, 1, at, :] = w * halo(1)
            side[c, 2, at, :] = w * halo(2)
            side[c, 3, at, :] = w * (halo(4) + ratio_of(scal, c) * film)
            side[c, 4, at, :] = halo(7)
            side[c, 5, at, :] = halo(6)
            side[c, 6, at, :] = halo(5)
            side[c, 7, at, :] = film
        return carry

    lax.fori_loop(0, total // rows, chunk, 0)

    def packed(c, first, at, count=4):
        result = jnp.zeros((at.stop - at.start, 128), f32)
        place = lax.broadcasted_iota(jnp.int32, result.shape, 1)
        for k in range(count):
            moved_in = pltpu.roll(side[c, first + k, at, :], 32 * k + COLS, 1)
            result = jnp.where((place >= 32 * k) & (place < 32 * k + 2 * COLS), moved_in, result)
        return result

    for c in range(2):
        for ref, at in ((up, slice(0, 32)), (down, slice(total - 32, total))):
            ref[c, 0:32, :] = packed(c, 0, at)
            ref[c, 32:64, :] = packed(c, 4, at)
            ref[c, 64:88, :] = packed(c, 7, slice(32, 56), 1)


def corner(ref, c, which, row, size):
    base, group = (64, 0) if which == 8 else (32 * (which // 4), which % 4)
    tile = ref[c, base + row : base + row + size, :]
    lane = lax.broadcasted_iota(jnp.int32, tile.shape, 1)
    tile = pltpu.roll(tile, 128 - COLS - 32 * group, 1)
    return jnp.where((lane < COLS) | (lane >= 128 - COLS), tile, 0.0)


def beside(main, extra):
    return jnp.concatenate([main, extra], axis=1)


def moved(stack, shift):
    size = stack.shape[0]
    return pltpu.roll(stack, size - shift, 0)[0 : size - 8]


def span(row, size):
    return slice(row, row + size) if isinstance(row, int) else pl.ds(pl.multiple_of(row, 8), size)


def chunks(first, last, body):
    count = (last - first) // 16

    def step(i, carry):
        body(first + pl.multiple_of(i * 16, 16))
        return carry

    lax.fori_loop(0, count, step, 0, unroll=2 if count % 2 == 0 else 1)


def split(value):
    high = value.astype(bf16)
    return high, (value - high.astype(f32)).astype(bf16)


def matrix(mats, size):
    if size == BLOCK:
        return mats[:, 0:480]
    return mats[0:64, 512:800] if size == 64 else mats[0:32, 896:1088]


def sweep(old, new, conv, mats, first, last, end, coefs, emit):
    lam, high, low = old
    start = first
    while start < last:
        size = BLOCK if last - start >= BLOCK else last - start
        near = slice(start - BAND, start + size + BAND)
        top = high[near, :]
        stack = jnp.concatenate([top, top, low[near, :]], axis=0)
        conv[0:size, :] = jnp.dot(matrix(mats, size), stack, preferred_element_type=f32)

        def chunk(row, start=start):
            w, wx, wy, wr = coefs(row)
            area = lam[span(row - 8, 32), :]
            mid = area[8:24]
            width = mid.shape[1]
            value = 0.2 * mid + wr
            value = value + wx * (area[7:23] + area[9:25])
            value = value + wy * (pltpu.roll(mid, 1, 1) + pltpu.roll(mid, width - 1, 1))
            value = value - w * conv[span(row - start, 16), :]
            emit(row, value, new)

        inner, outer = max(start, HALO), min(start + size, end)
        for row in range(start, min(start + size, HALO), 16):
            chunk(row)
        for row in range(inner, outer, 16):
            chunk(row)
        for row in range(max(start, end), start + size, 16):
            chunk(row)
        start += size


def keep(row, value, new):
    lam, high, low = new
    at = span(row, 16)
    lam[at, :] = value
    high[at, :], low[at, :] = split(value)


def send_edges(lam_out, up, down):
    total = lam_out.shape[0]
    up[...] = lam_out[0:HALO, :]
    down[...] = lam_out[total - HALO : total, :]


def first_kernel(c, scal, mats, coef, side, lam_in, film, top, bot, top_corner, bot_corner, *rest):
    if c:
        grad_in, *rest = rest
    lam_out, up, down, grad, coef_top, coef_bot, la, ha, oa, lb, hb, ob, conv = rest
    total = lam_in.shape[1]
    cols = grad.shape[1]
    end = HALO + total
    top_ok = scal[6].astype(f32)
    low_ok = scal[7].astype(f32)
    r = ratio_of(scal, c)
    for ref, edge, ok, out, base in (
        (top, top_corner, top_ok, coef_top, HALO - COEF),
        (bot, bot_corner, low_ok, coef_bot, end),
    ):
        for row in range(0, COEF, 16):
            w = ok * (0.8 / ref[c, row : row + 16, :])
            fx = w * ref[c, 32 + row : 48 + row, :]
            fy = w * ref[c, 64 + row : 80 + row, :]
            lam = w * (ref[c, 96 + row : 112 + row, :] + r * ref[c, 128 + row : 144 + row, :])
            for k, main in enumerate((w, fx, fy)):
                out[k, row : row + 16, :] = beside(main, ok * corner(edge, c, k, row, 16))
            keep(base + row, beside(lam, ok * corner(edge, c, 3, row, 16)), (la, ha, oa))

    def load(row):
        at = span(row - HALO, 16)
        keep(row, beside(lam_in[c, at, :], side[c, 3, at, :]), (la, ha, oa))

    chunks(HALO, end, load)

    def coefs(row):
        if isinstance(row, int) and not HALO <= row < end:
            ref, at = (coef_top, row - HALO + COEF) if row < HALO else (coef_bot, row - end)
            return (*[ref[k, at : at + 16, :] for k in range(3)], la[row : row + 16, :])
        at = span(row - HALO, 16)
        parts = [beside(coef[c, k, at, :], side[c, k, at, :]) for k in range(3)]
        return (*parts, beside(lam_in[c, at, :], side[c, 3, at, :]))

    sweep((la, ha, oa), (lb, hb, ob), conv, mats, HALO - 16, end + 16, end, coefs, keep)

    def emit(row, value, new):
        at = span(row - HALO, 16)
        lam_out[at, :] = value
        term = value[:, 0:cols] * film[c, at, :]
        grad[at, :] = grad_in[at, :] + term if c else term

    sweep((lb, hb, ob), None, conv, mats, HALO, end, end, coefs, emit)
    send_edges(lam_out, up, down)


def step_kernel(
    step, c, scal, mats, coef, side, coef_top, coef_bot, top_corner, bot_corner,
    src, src_top, src_bot, lam_in, lam_top, lam_bot, film, grad_in, *rest,
):
    final = step == 0
    if step == 2:
        film_top, film_bot, *rest = rest
    if final:
        if c:
            _, _, *rest = rest
            lam_full, film_full, mine, other, film_now, lam_out, film_out, grad, *rest = rest
        else:
            lam_full, film_full, grad, film_now, lam_out, film_out, *rest = rest
        sems, *rest = rest
    else:
        lam_out, up, down, film_now, grad, *rest = rest
    la, ha, oa, lb, hb, ob, wr_ref, conv = rest
    total = lam_in.shape[0]
    cols = grad.shape[1]
    end = HALO + total
    top_ok = scal[6].astype(f32)
    low_ok = scal[7].astype(f32)
    reach = 8 * step
    r = ratio_of(scal, c)

    def old_film(row, size):
        if step < 2:
            return film[span(row - (HALO - COEF), size), :]
        if not isinstance(row, int):
            at = span(row - HALO, size)
            return beside(film[c, at, :], side[c, 7, at, :])
        parts = []
        for k in range(row, row + size, 8):
            if k < HALO:
                at = k - HALO + COEF
                part = top_ok * beside(film_top[c, 128 + at : 136 + at, :], corner(top_corner, c, 7, at, 8))
            elif k < end:
                at = slice(k - HALO, k - HALO + 8)
                part = beside(film[c, at, :], side[c, 7, at, :])
            elif k < end + 32:
                at = k - end
                part = low_ok * beside(film_bot[c, 128 + at : 136 + at, :], corner(bot_corner, c, 7, at, 8))
            else:
                at = k - end - 32
                part = low_ok * beside(src_bot[c, 32 + at : 40 + at, :], corner(bot_corner, c, 8, at, 8))
            parts.append(part)
        return jnp.concatenate(parts, axis=0)

    def coef_at(row, k):
        if isinstance(row, int) and not HALO <= row < end:
            ref, at = (coef_top, row - HALO + COEF) if row < HALO else (coef_bot, row - end)
            return ref[k, at : at + 16, :]
        at = span(row - HALO, 16)
        return beside(coef[c, k, at, :], side[c, k, at, :])

    def source(row):
        if isinstance(row, int) and not HALO <= row < end:
            ref, edge, at = (src_top, top_corner, row - HALO + COEF) if row < HALO else (src_bot, bot_corner, row - end)
            here = 32 * (step % 2) + at
            return beside(ref[c, here : here + 16, :], corner(edge, c, 4 + step, at, 16))
        at = span(row - HALO, 16)
        return beside(src[c, step, at, :], side[c, 4 + step, at, :])

    shift = scal[step + 1]

    def begin(row):
        if isinstance(row, int) and row < HALO:
            lam = lam_top[row : row + 16, :] * top_ok
        elif isinstance(row, int) and row >= end:
            lam = lam_bot[row - end : row - end + 16, :] * low_ok
        else:
            lam = lam_in[span(row - HALO, 16), :]
        keep(row, lam, (la, ha, oa))
        height = 16
        if isinstance(row, int):
            if row < HALO - COEF or row >= end + COEF + reach:
                return
            height = min(16, end + COEF + reach - row)
        now = moved(old_film(row, height + 8), shift) + r * lam[0:height]
        at = row - HALO + COEF
        film_now[span(at, height), :] = now
        if not isinstance(row, int) or row < end + COEF:
            wr_ref[span(at, 16), :] = coef_at(row, 0) * (source(row) + r * now)

    for row in range(0, HALO, 16):
        begin(row)
    chunks(HALO, end - 32, begin)
    for row in range(end - 32, end + HALO, 16):
        begin(row)

    def coefs(row):
        return coef_at(row, 0), coef_at(row, 1), coef_at(row, 2), wr_ref[span(row - HALO + COEF, 16), :]

    a, b = (la, ha, oa), (lb, hb, ob)
    sweep(a, b, conv, mats, HALO - 32, end + 32, end, coefs, keep)
    sweep(b, a, conv, mats, HALO - 16, end + 16, end, coefs, keep)

    def emit(row, value, new):
        at = span(row - HALO, 16)
        here = row - HALO + COEF
        grad[at, :] = grad_in[at, :] + value[:, 0:cols] * film_now[span(here, 16), 0:cols]
        if final:
            lam_out[at, :] = value[:, 0:cols]
            film_out[at, :] = moved(film_now[span(here, 24), 0:cols], scal[0]) + r * value[:, 0:cols]
        else:
            lam_out[at, :] = value

    sweep(a, None, conv, mats, HALO, end, end, coefs, emit)
    if final:
        run_copies([(lam_out, lam_full.at[c]), (film_out, film_full.at[c])], sems)
        if c:
            half = total // 2
            first = pl.multiple_of(scal[10] * half, half)
            mine[...] = grad[pl.ds(first, half), :]
            other[...] = grad[pl.ds(pl.multiple_of(half - first, half), half), :]
    else:
        send_edges(lam_out, up, down)


VM = pl.BlockSpec(memory_space=pltpu.VMEM)
SM = pl.BlockSpec(memory_space=pltpu.SMEM)
HB = pl.BlockSpec(memory_space=pltpu.HBM)


def call(body, smem, vmem, outs, scratch=(), flops=0, name=None, space=VM, limit=12, hbm_outs=0, hbm_ins=0):
    moved_bytes = sum(v.size * 4 for v in vmem) + sum(4 * functools.reduce(lambda a, b: a * b, o.shape) for o in outs)
    return pl.pallas_call(
        body,
        out_shape=tuple(outs),
        in_specs=[SM] * len(smem) + [space] * (len(vmem) - hbm_ins) + [HB] * hbm_ins,
        out_specs=tuple([HB] * hbm_outs + [VM] * (len(outs) - hbm_outs)),
        input_output_aliases={len(smem) + len(vmem) - hbm_ins + i: i for i in range(hbm_ins)},
        scratch_shapes=list(scratch),
        cost_estimate=pl.CostEstimate(flops=flops, bytes_accessed=moved_bytes, transcendentals=0),
        compiler_params=pltpu.CompilerParams(vmem_limit_bytes=limit << 20),
        name=name,
    )(*smem, *[pltpu.with_memory_space_constraint(v, pltpu.HBM) for v in vmem] if space is HB else vmem)


def ring(axis, step):
    count = lax.axis_size(axis)
    return [(i, (i + step) % count) for i in range(count)]


def both_ways(up, down, axis):
    from_high = lax.ppermute(up, axis, ring(axis, -1))
    from_low = lax.ppermute(down, axis, ring(axis, 1))
    return from_low, from_high


def after(values, gate):
    return lax.optimization_barrier((tuple(values), tuple(gate)))[0]


def case_sum(mine, other, core):
    swap_core = [(i, i ^ 1) for i in range(4)]
    swap_chip = [(i, i ^ 2) for i in range(4)]
    mine = mine + lax.ppermute(other, "case", swap_core)
    mine = mine + lax.ppermute(mine, "case", swap_chip)
    other = lax.ppermute(mine, "case", swap_core)
    return jnp.where(
        core == 0, jnp.concatenate([mine, other], axis=0), jnp.concatenate([other, mine], axis=0)
    )


def on_device(ratio_index, shifts, kernel, diagonal, flow_x, flow_y, pres_source, rough_adjoint):
    cases, total, cols = diagonal.shape
    wide = cols + 128
    roll, trans = lax.axis_index("roll"), lax.axis_index("trans")
    core = lax.axis_index("case") % 2
    scal = jnp.concatenate(
        [
            shifts,
            ratio_index,
            jnp.stack(
                [
                    (roll > 0).astype(jnp.int32),
                    (roll < lax.axis_size("roll") - 1).astype(jnp.int32),
                    (trans > 0).astype(jnp.int32),
                    (trans < lax.axis_size("trans") - 1).astype(jnp.int32),
                    core,
                ]
            ),
        ]
    )

    def shape(*dims, dtype=f32):
        return jax.ShapeDtypeStruct(dims, dtype)

    raw = (diagonal, flow_x, flow_y, rough_adjoint, pres_source)
    edges = call(
        edges_kernel,
        (scal,),
        raw,
        [shape(cases, rows, cols) for rows in (160, 160, 56, 32, 64, 64)],
        [pltpu.SemaphoreType.DMA((34,))],
        name="edges",
        space=HB,
    )
    near = both_ways(edges[0], edges[1], "roll")
    (scal,) = after((scal,), (edges[0],))
    tile = pltpu.VMEM((SLOTS, cases, total, 128), f32)
    left, right = call(
        pack_kernel,
        (scal,),
        raw,
        [shape(cases, total, 128)] * 2,
        [tile, tile, pltpu.SemaphoreType.DMA((2 * SLOTS,))],
        name="pack",
        space=HB,
    )
    from_left, from_right = both_ways(left, right, "trans")
    (mats,) = call(bands_kernel, (kernel,), (left,), [shape(BLOCK, 1152, dtype=bf16)], name="bands")
    coef, lam = call(
        main_kernel,
        (scal,),
        raw,
        [shape(cases, 3, total, cols), shape(cases, total, cols)],
        name="main",
    )
    from_left, from_right = after((from_left, from_right), (coef, mats))
    side, up, down = call(
        side_kernel,
        (scal,),
        (from_left, from_right),
        [shape(cases, 8, total, 128), shape(cases, 88, 128), shape(cases, 88, 128)],
        name="side",
    )
    top_corner, bot_corner = both_ways(up, down, "roll")
    rows = total + 2 * HALO
    fields = [pltpu.VMEM((rows, wide), f32), pltpu.VMEM((rows, wide), bf16), pltpu.VMEM((rows, wide), bf16)]
    conv = pltpu.VMEM((BLOCK, wide), f32)
    work = [*fields, *fields, pltpu.VMEM((total + 2 * COEF, wide), f32), conv]
    state = [shape(total, wide), shape(HALO, wide), shape(HALO, wide)]
    halo = shape(3, COEF, wide)
    block = shape(total, cols)
    grad = None
    lams, ends, coefs, films = [None] * 2, [None] * 2, [None] * 2, [rough_adjoint] * 2
    for c in range(2):
        lams[c], up, down, grad, *coefs[c] = call(
            functools.partial(first_kernel, c),
            (scal,),
            (mats, coef, side, lam, rough_adjoint, *near, top_corner, bot_corner, *([grad] if c else [])),
            [*state, block, halo, halo],
            [*fields, *fields, conv],
            flops=1 << 30,
            name="first" + str(c),
        )
        ends[c] = both_ways(up, down, "roll")
        if c == 0:
            later = both_ways(*after(edges[2:4], lams[:1]), "roll")
    out = ()
    for step in range(STEPS - 2, -1, -1):
        for c in range(2):
            film = shape(total + 2 * COEF + 8 * step, wide)
            scratch = work
            hbm_outs = hbm_ins = 0
            if step:
                outs = [*state, film, block]
            else:
                full = shape(cases, total, cols)
                half = shape(total // 2, cols)
                outs = [full, full, half, half] if c else [full, full, block]
                kept = [film, block, block] + ([block] if c else [])
                scratch = [*[pltpu.VMEM(k.shape, f32) for k in kept], pltpu.SemaphoreType.DMA((2,)), *work]
                hbm_outs, hbm_ins = 2, 2 * c
            more = near if step == 2 else out
            result = call(
                functools.partial(step_kernel, step, c),
                (scal,),
                (
                    mats, coef, side, *coefs[c], top_corner, bot_corner, pres_source, *(later if step == 2 else last),
                    lams[c], *ends[c], films[c], grad, *more,
                ),
                outs,
                scratch,
                flops=3 << 29,
                name="step" + str(step) + "case" + str(c),
                hbm_outs=hbm_outs,
                hbm_ins=hbm_ins,
            )
            if step:
                lams[c], up, down, films[c], grad = result
                ends[c] = both_ways(up, down, "roll")
                if step == STEPS - 2 and c == 0:
                    last = both_ways(*after(edges[4:6], lams[:1]), "roll")
            elif c == 0:
                *out, grad = result
            else:
                lam, film, mine, other = result
    return lam, film, case_sum(mine, other, core)


def solution(mesh):
    block = P("case", "roll", "trans")
    in_specs = (P("case"), P(), P(), block, block, block, P("case", None, "roll", "trans"), block)
    out_specs = (block, block, P("roll", "trans"))
    return jax.shard_map(on_device, mesh=mesh, in_specs=in_specs, out_specs=out_specs, check_vma=False)
```

```python
import functools

import jax
import jax.numpy as jnp
from jax import lax
from jax.experimental import pallas as pl
from jax.experimental.pallas import tpu as pltpu
from jax.sharding import PartitionSpec as P

STEPS = 4
SWEEPS = 3
KERN = 31
NSRR = 16
HALO = 48
COEF = 32
COLS = STEPS * SWEEPS - 1
BAND = 16
BLOCK = 128
SLOTS = 8

f32 = jnp.float32
bf16 = jnp.bfloat16


def banded(kern_ref, rows):
    width = rows + 2 * BAND
    shape = (rows, 3 * width)
    lane = lax.broadcasted_iota(jnp.int32, shape, 1)
    part = (lane >= width).astype(jnp.int32) + (lane >= 2 * width).astype(jnp.int32)
    tap = lane - part * width - lax.broadcasted_iota(jnp.int32, shape, 0) - 1
    value = jnp.zeros(shape, f32)
    for k in range(KERN):
        value = jnp.where(tap == k, kern_ref[k], value)
    high = value.astype(bf16).astype(f32)
    return jnp.where(part == 1, value - high, high).astype(bf16)


def bands_kernel(kern_ref, gate, mats):
    mats[:, 0:480] = banded(kern_ref, BLOCK)
    mats[0:64, 512:800] = banded(kern_ref, 64)
    mats[0:32, 896:1088] = banded(kern_ref, 32)


def run_copies(pairs, sems):
    copies = [pltpu.make_async_copy(a, b, sems.at[i]) for i, (a, b) in enumerate(pairs)]
    for copy in copies:
        copy.start()
    for copy in copies:
        copy.wait()


def edges_kernel(scal, diag, fx, fy, film, src, up_a, down_a, up_b, down_b, up_c, down_c, sems):
    total = diag.shape[1]
    low, high = slice(0, COEF), slice(total - COEF, total)
    pairs = []
    for edge, a, b, c in ((low, up_a, up_b, up_c), (high, down_a, down_b, down_c)):
        for k, ref in enumerate((diag, fx, fy, src.at[:, STEPS - 1], film)):
            pairs.append((ref.at[:, edge], a.at[:, 32 * k : 32 * k + 32]))
        pairs.append((src.at[:, 2, edge], b.at[:, 0:32]))
        pairs.append((src.at[:, 1, edge], c.at[:, 0:32]))
        pairs.append((src.at[:, 0, edge], c.at[:, 32:64]))
    pairs.append((film.at[:, 32:56], up_b.at[:, 32:56]))
    run_copies(pairs, sems)


def pack_kernel(scal, diag, fx, fy, film, src, left, right, low, high, sems):
    total, cols = diag.shape[1], diag.shape[2]
    refs = [diag, fx, fy, film] + [src.at[:, s] for s in (3, 2, 1, 0)]
    pairs = []
    for slot, ref in enumerate(refs):
        pairs.append((ref.at[:, :, 0:128], low.at[slot]))
        pairs.append((ref.at[:, :, cols - 128 : cols], high.at[slot]))
    run_copies(pairs, sems)
    rows = 32
    lane = lax.broadcasted_iota(jnp.int32, (rows, 128), 1)

    def chunk(i, carry):
        at = pl.ds(pl.multiple_of(i * rows, rows), rows)
        for c in range(2):
            first = jnp.zeros((rows, 128), f32)
            last = jnp.zeros((rows, 128), f32)
            for slot in range(SLOTS):
                place = COLS * slot
                here = (lane >= place) & (lane < place + COLS)
                a, b = low[slot, c, at, :], high[slot, c, at, :]
                first = jnp.where(here, pltpu.roll(a, place, 1) if place else a, first)
                last = jnp.where(here, pltpu.roll(b, (place + COLS) % 128, 1), last)
            left[c, at, :] = first
            right[c, at, :] = last
        return carry

    lax.fori_loop(0, total // rows, chunk, 0)


def ratio_of(scal, c):
    return 0.2 + 1.6 * scal[4 + c].astype(f32) / (NSRR - 1)


def main_kernel(scal, diag, fx, fy, film, src, coef, lam):
    rows = 16

    def chunk(i, carry):
        at = pl.ds(pl.multiple_of(i * rows, rows), rows)
        for c in range(2):
            w = 0.8 / diag[c, at, :]
            coef[c, 0, at, :] = w
            coef[c, 1, at, :] = w * fx[c, at, :]
            coef[c, 2, at, :] = w * fy[c, at, :]
            lam[c, at, :] = w * (src[c, STEPS - 1, at, :] + ratio_of(scal, c) * film[c, at, :])
        return carry

    lax.fori_loop(0, diag.shape[1] // rows, chunk, 0)


def side_kernel(scal, from_left, from_right, side, up, down):
    total = side.shape[2]
    rows = 32
    lane = lax.broadcasted_iota(jnp.int32, (rows, 128), 1)
    is_right = lane < COLS
    inside = (is_right & (scal[9] > 0)) | ((lane >= 128 - COLS) & (scal[8] > 0))

    def chunk(i, carry):
        at = pl.ds(pl.multiple_of(i * rows, rows), rows)
        for c in range(2):
            lo = from_left[c, at, :]
            hi = from_right[c, at, :]

            def halo(slot):
                place = COLS * slot
                right = pltpu.roll(hi, (128 - place) % 128, 1) if place else hi
                left = pltpu.roll(lo, (128 - COLS - place) % 128, 1)
                return jnp.where(inside, jnp.where(is_right, right, left), 0.0)

            w = jnp.where(inside, 0.8 / jnp.where(inside, halo(0), 1.0), 0.0)
            film = halo(3)
            side[c, 0, at, :] = w
            side[c, 1, at, :] = w * halo(1)
            side[c, 2, at, :] = w * halo(2)
            side[c, 3, at, :] = w * (halo(4) + ratio_of(scal, c) * film)
            side[c, 4, at, :] = halo(7)
            side[c, 5, at, :] = halo(6)
            side[c, 6, at, :] = halo(5)
            side[c, 7, at, :] = film
        return carry

    lax.fori_loop(0, total // rows, chunk, 0)

    def packed(c, first, at, count=4):
        result = jnp.zeros((at.stop - at.start, 128), f32)
        place = lax.broadcasted_iota(jnp.int32, result.shape, 1)
        for k in range(count):
            moved_in = pltpu.roll(side[c, first + k, at, :], 32 * k + COLS, 1)
            result = jnp.where((place >= 32 * k) & (place < 32 * k + 2 * COLS), moved_in, result)
        return result

    for c in range(2):
        for ref, at in ((up, slice(0, 32)), (down, slice(total - 32, total))):
            ref[c, 0:32, :] = packed(c, 0, at)
            ref[c, 32:64, :] = packed(c, 4, at)
            ref[c, 64:88, :] = packed(c, 7, slice(32, 56), 1)


def corner(ref, c, which, row, size):
    base, group = (64, 0) if which == 8 else (32 * (which // 4), which % 4)
    tile = ref[c, base + row : base + row + size, :]
    lane = lax.broadcasted_iota(jnp.int32, tile.shape, 1)
    tile = pltpu.roll(tile, 128 - COLS - 32 * group, 1)
    return jnp.where((lane < COLS) | (lane >= 128 - COLS), tile, 0.0)


def beside(main, extra):
    return jnp.concatenate([main, extra], axis=1)


def moved(near, shift):
    stack = jnp.concatenate(near, axis=0)
    size = stack.shape[0]
    return pltpu.roll(stack, size - shift, 0)[0 : size - 8]


def split(value):
    high = value.astype(bf16)
    return high, (value - high.astype(f32)).astype(bf16)


def matrix(mats, size):
    if size == BLOCK:
        return mats[:, 0:480]
    return mats[0:64, 512:800] if size == 64 else mats[0:32, 896:1088]


def sweep(old, new, conv, mats, first, last, coefs, emit):
    lam, high, low = old
    start = first
    while start < last:
        size = BLOCK if last - start >= BLOCK else last - start
        near = slice(start - BAND, start + size + BAND)
        top = high[near, :]
        stack = jnp.concatenate([top, top, low[near, :]], axis=0)
        conv[0:size, :] = jnp.dot(matrix(mats, size), stack, preferred_element_type=f32)
        for row in range(start, start + size, 16):
            w, wx, wy, wr = coefs(row)
            area = lam[row - 8 : row + 24, :]
            mid = area[8:24]
            width = mid.shape[1]
            value = 0.2 * mid + wr
            value = value + wx * (area[7:23] + area[9:25])
            value = value + wy * (pltpu.roll(mid, 1, 1) + pltpu.roll(mid, width - 1, 1))
            value = value - w * conv[row - start : row - start + 16, :]
            emit(row, value, new)
        start += size


def keep(row, value, new):
    lam, high, low = new
    at = slice(row, row + 16)
    lam[at, :] = value
    high[at, :], low[at, :] = split(value)


def first_kernel(
    scal, mats, coef, side, lam_in, film, top, bot, top_corner, bot_corner,
    lam_out, up, down, grad, coef_top, coef_bot, la, ha, oa, lb, hb, ob, conv,
):
    total = lam_in.shape[1]
    cols = grad.shape[1]
    end = HALO + total
    top_ok = scal[6].astype(f32)
    low_ok = scal[7].astype(f32)

    def case(c, carry):
        r = ratio_of(scal, c)
        for ref, edge, ok, out, base in (
            (top, top_corner, top_ok, coef_top, HALO - COEF),
            (bot, bot_corner, low_ok, coef_bot, end),
        ):
            for row in range(0, COEF, 16):
                w = ok * (0.8 / ref[c, row : row + 16, :])
                fx = w * ref[c, 32 + row : 48 + row, :]
                fy = w * ref[c, 64 + row : 80 + row, :]
                lam = w * (ref[c, 96 + row : 112 + row, :] + r * ref[c, 128 + row : 144 + row, :])
                for k, main in enumerate((w, fx, fy)):
                    out[c, k, row : row + 16, :] = beside(main, ok * corner(edge, c, k, row, 16))
                keep(base + row, beside(lam, ok * corner(edge, c, 3, row, 16)), (la, ha, oa))
        for row in range(HALO, end, 16):
            at = slice(row - HALO, row - HALO + 16)
            keep(row, beside(lam_in[c, at, :], side[c, 3, at, :]), (la, ha, oa))

        def coefs(row):
            if row < HALO:
                at = slice(row - HALO + COEF, row - HALO + COEF + 16)
                return (*[coef_top[c, k, at, :] for k in range(3)], None)
            if row >= end:
                at = slice(row - end, row - end + 16)
                return (*[coef_bot[c, k, at, :] for k in range(3)], None)
            at = slice(row - HALO, row - HALO + 16)
            return (*[beside(coef[c, k, at, :], side[c, k, at, :]) for k in range(3)], None)

        def with_rhs(row):
            if HALO <= row < end:
                at = slice(row - HALO, row - HALO + 16)
                return (*coefs(row)[:3], beside(lam_in[c, at, :], side[c, 3, at, :]))
            return (*coefs(row)[:3], la[row : row + 16, :])

        sweep((la, ha, oa), (lb, hb, ob), conv, mats, HALO - 16, end + 16, with_rhs, keep)

        def emit(row, value, new):
            at = slice(row - HALO, row - HALO + 16)
            lam_out[c, at, :] = value
            if row < HALO + HALO:
                up[c, at, :] = value
            if row >= end - HALO:
                down[c, row - end + HALO : row - end + HALO + 16, :] = value
            term = value[:, 0:cols] * film[c, at, :]
            grad[at, :] = jnp.where(c == 0, term, grad[at, :] + term)

        sweep((lb, hb, ob), None, conv, mats, HALO, end, with_rhs, emit)
        return carry

    lax.fori_loop(0, 2, case, 0)


def step_kernel(
    step, scal, mats, coef, side, coef_top, coef_bot, top_corner, bot_corner,
    src, src_top, src_bot, lam_in, lam_top, lam_bot, film, *rest,
):
    final = step == 0
    if step == 2:
        film_top, film_bot, *rest = rest
    grad_in, *rest = rest
    if final:
        lam_out, film_out, mine, other, film_now, grad, *rest = rest
    else:
        lam_out, up, down, film_now, grad, *rest = rest
    la, ha, oa, lb, hb, ob, wr_ref, conv = rest
    total = lam_in.shape[1]
    cols = grad.shape[1]
    end = HALO + total
    top_ok = scal[6].astype(f32)
    low_ok = scal[7].astype(f32)
    reach = 8 * step
    place = {2: 0, 1: 0, 0: 32}[step]

    def case(c, carry):
        r = ratio_of(scal, c)

        def old_film(row):
            if step < 2:
                at = row - (HALO - COEF)
                return film[c, at : at + 8, :]
            if row < HALO:
                at = row - HALO + COEF
                return top_ok * beside(film_top[c, 128 + at : 136 + at, :], corner(top_corner, c, 7, at, 8))
            if row < end:
                at = slice(row - HALO, row - HALO + 8)
                return beside(film[c, at, :], side[c, 7, at, :])
            at = row - end
            if at < 32:
                return low_ok * beside(film_bot[c, 128 + at : 136 + at, :], corner(bot_corner, c, 7, at, 8))
            return low_ok * beside(src_bot[c, at : at + 8, :], corner(bot_corner, c, 8, at - 32, 8))

        def coef_at(row, k):
            if row < HALO:
                return coef_top[c, k, row - HALO + COEF : row - HALO + COEF + 16, :]
            if row >= end:
                return coef_bot[c, k, row - end : row - end + 16, :]
            at = slice(row - HALO, row - HALO + 16)
            return beside(coef[c, k, at, :], side[c, k, at, :])

        def source(row):
            if row < HALO:
                at = row - HALO + COEF
                return beside(src_top[c, place + at : place + at + 16, :], corner(top_corner, c, 4 + step, at, 16))
            if row >= end:
                at = row - end
                return beside(src_bot[c, place + at : place + at + 16, :], corner(bot_corner, c, 4 + step, at, 16))
            at = slice(row - HALO, row - HALO + 16)
            return beside(src[c, step, at, :], side[c, 4 + step, at, :])

        shift = scal[step + 1]
        for row in range(0, end + HALO, 16):
            if row < HALO:
                lam = lam_top[c, row : row + 16, :] * top_ok
            elif row >= end:
                lam = lam_bot[c, row - end : row - end + 16, :] * low_ok
            else:
                lam = lam_in[c, row - HALO : row - HALO + 16, :]
            keep(row, lam, (la, ha, oa))
            if row < HALO - COEF or row >= end + COEF + reach:
                continue
            height = 16 if row + 16 <= end + COEF + reach else 8
            near = [old_film(row + k) for k in range(0, height + 8, 8)]
            now = moved(near, shift) + r * lam[0:height]
            at = row - HALO + COEF
            film_now[c, at : at + height, :] = now
            if row < end + COEF:
                wr_ref[at : at + 16, :] = coef_at(row, 0) * (source(row) + r * now)

        def coefs(row):
            at = row - HALO + COEF
            return coef_at(row, 0), coef_at(row, 1), coef_at(row, 2), wr_ref[at : at + 16, :]

        a, b = (la, ha, oa), (lb, hb, ob)
        sweep(a, b, conv, mats, HALO - 32, end + 32, coefs, keep)
        sweep(b, a, conv, mats, HALO - 16, end + 16, coefs, keep)

        def emit(row, value, new):
            at = slice(row - HALO, row - HALO + 16)
            here = slice(row - HALO + COEF, row - HALO + COEF + 16)
            term = value[:, 0:cols] * film_now[c, here, 0:cols]
            grad[at, :] = jnp.where(c == 0, grad_in[at, :], grad[at, :]) + term
            if final:
                lam_out[c, at, :] = value[:, 0:cols]
                near = [film_now[c, here.start + k : here.start + k + 8, 0:cols] for k in range(0, 24, 8)]
                film_out[c, at, :] = moved(near, scal[0]) + r * value[:, 0:cols]
                return
            lam_out[c, at, :] = value
            if row < HALO + HALO:
                up[c, at, :] = value
            if row >= end - HALO:
                down[c, row - end + HALO : row - end + HALO + 16, :] = value

        sweep(a, None, conv, mats, HALO, end, coefs, emit)
        return carry

    lax.fori_loop(0, 2, case, 0)
    if final:
        half = total // 2
        first = pl.multiple_of(scal[10] * half, half)
        mine[...] = grad[pl.ds(first, half), :]
        other[...] = grad[pl.ds(pl.multiple_of(half - first, half), half), :]


VM = pl.BlockSpec(memory_space=pltpu.VMEM)
SM = pl.BlockSpec(memory_space=pltpu.SMEM)
HB = pl.BlockSpec(memory_space=pltpu.HBM)


def call(body, smem, vmem, outs, scratch=(), flops=0, name=None, space=VM, limit=12):
    moved_bytes = sum(v.size * 4 for v in vmem) + sum(4 * functools.reduce(lambda a, b: a * b, o.shape) for o in outs)
    return pl.pallas_call(
        body,
        out_shape=tuple(outs),
        in_specs=[SM] * len(smem) + [space] * len(vmem),
        out_specs=tuple([VM] * len(outs)),
        scratch_shapes=list(scratch),
        cost_estimate=pl.CostEstimate(flops=flops, bytes_accessed=moved_bytes, transcendentals=0),
        compiler_params=pltpu.CompilerParams(vmem_limit_bytes=limit << 20),
        name=name,
    )(*smem, *[pltpu.with_memory_space_constraint(v, pltpu.HBM) for v in vmem] if space is HB else vmem)


def ring(axis, step):
    count = lax.axis_size(axis)
    return [(i, (i + step) % count) for i in range(count)]


def both_ways(up, down, axis):
    from_high = lax.ppermute(up, axis, ring(axis, -1))
    from_low = lax.ppermute(down, axis, ring(axis, 1))
    return from_low, from_high


def after(values, gate):
    return lax.optimization_barrier((tuple(values), tuple(gate)))[0]


def case_sum(mine, other, core):
    swap_core = [(i, i ^ 1) for i in range(4)]
    swap_chip = [(i, i ^ 2) for i in range(4)]
    mine = mine + lax.ppermute(other, "case", swap_core)
    mine = mine + lax.ppermute(mine, "case", swap_chip)
    other = lax.ppermute(mine, "case", swap_core)
    return jnp.where(
        core == 0, jnp.concatenate([mine, other], axis=0), jnp.concatenate([other, mine], axis=0)
    )


def on_device(ratio_index, shifts, kernel, diagonal, flow_x, flow_y, pres_source, rough_adjoint):
    cases, total, cols = diagonal.shape
    wide = cols + 128
    roll, trans = lax.axis_index("roll"), lax.axis_index("trans")
    core = lax.axis_index("case") % 2
    scal = jnp.concatenate(
        [
            shifts,
            ratio_index,
            jnp.stack(
                [
                    (roll > 0).astype(jnp.int32),
                    (roll < lax.axis_size("roll") - 1).astype(jnp.int32),
                    (trans > 0).astype(jnp.int32),
                    (trans < lax.axis_size("trans") - 1).astype(jnp.int32),
                    core,
                ]
            ),
        ]
    )

    def shape(*dims, dtype=f32):
        return jax.ShapeDtypeStruct(dims, dtype)

    raw = (diagonal, flow_x, flow_y, rough_adjoint, pres_source)
    up_a, down_a, up_b, down_b, up_c, down_c = call(
        edges_kernel,
        (scal,),
        raw,
        [shape(cases, rows, cols) for rows in (160, 160, 56, 32, 64, 64)],
        [pltpu.SemaphoreType.DMA((17,))],
        name="edges",
        space=HB,
    )
    top_a, bot_a = both_ways(up_a, down_a, "roll")
    tile = pltpu.VMEM((SLOTS, cases, total, 128), f32)
    left, right = call(
        pack_kernel,
        (scal,),
        raw,
        [shape(cases, total, 128)] * 2,
        [tile, tile, pltpu.SemaphoreType.DMA((2 * SLOTS,))],
        name="pack",
        space=HB,
    )
    from_left, from_right = both_ways(left, right, "trans")
    (mats,) = call(bands_kernel, (kernel,), (left,), [shape(BLOCK, 1152, dtype=bf16)], name="bands")
    coef, lam = call(
        main_kernel,
        (scal,),
        raw,
        [shape(cases, 3, total, cols), shape(cases, total, cols)],
        name="main",
    )
    from_left, from_right = after((from_left, from_right), (coef, mats))
    side, up, down = call(
        side_kernel,
        (scal,),
        (from_left, from_right),
        [shape(cases, 8, total, 128), shape(cases, 88, 128), shape(cases, 88, 128)],
        name="side",
    )
    top_corner, bot_corner = both_ways(up, down, "roll")
    up_b, down_b = after((up_b, down_b), (top_a, bot_a))
    top_b, bot_b = both_ways(up_b, down_b, "roll")

    rows = total + 2 * HALO
    fields = [pltpu.VMEM((rows, wide), f32), pltpu.VMEM((rows, wide), bf16), pltpu.VMEM((rows, wide), bf16)]
    conv = pltpu.VMEM((BLOCK, wide), f32)
    work = [*fields, *fields, pltpu.VMEM((total + 2 * COEF, wide), f32), conv]
    state = [shape(cases, total, wide), shape(cases, HALO, wide), shape(cases, HALO, wide)]
    lam, up, down, grad, coef_top, coef_bot = call(
        first_kernel,
        (scal,),
        (mats, coef, side, lam, rough_adjoint, top_a, bot_a, top_corner, bot_corner),
        [*state, shape(total, cols), shape(cases, 3, COEF, wide), shape(cases, 3, COEF, wide)],
        [*fields, *fields, conv],
        flops=2 << 30,
        name="first",
    )
    film = rough_adjoint
    for step in range(STEPS - 2, -1, -1):
        lam_top, lam_bot = both_ways(up, down, "roll")
        src_top, src_bot = (top_b, bot_b) if step == 2 else last
        films = shape(cases, total + 2 * COEF + 8 * step, wide)
        half = shape(total // 2, cols)
        if step:
            outs = [*state, films, shape(total, cols)]
            scratch = work
        else:
            outs = [shape(cases, total, cols), shape(cases, total, cols), half, half]
            scratch = [pltpu.VMEM(films.shape, f32), pltpu.VMEM((total, cols), f32), *work]
        more = (top_a, bot_a) if step == 2 else ()
        result = call(
            functools.partial(step_kernel, step),
            (scal,),
            (
                mats, coef, side, coef_top, coef_bot, top_corner, bot_corner, pres_source, src_top, src_bot,
                lam, lam_top, lam_bot, film, *more, grad,
            ),
            outs,
            scratch,
            flops=3 << 30,
            name="step" + str(step),
        )
        if step:
            lam, up, down, film, grad = result
            if step == STEPS - 2:
                last = both_ways(*after((up_c, down_c), (lam,)), "roll")
        else:
            lam, film, mine, other = result
    return lam, film, case_sum(mine, other, core)


def solution(mesh):
    block = P("case", "roll", "trans")
    in_specs = (P("case"), P(), P(), block, block, block, P("case", None, "roll", "trans"), block)
    out_specs = (block, block, P("roll", "trans"))
    return jax.shard_map(on_device, mesh=mesh, in_specs=in_specs, out_specs=out_specs, check_vma=False)
```
